256 devices in a mesh: ctx: 4 (over z_hi), head: 32 (over y, x, core), rep: 2 (over z_lo).
Axes of the slice: x: 4, y: 4, z: 8 (z_hi: 4, z_lo: 2; z = z_hi * 2 + z_lo), core: 2. Of those that a mesh axis runs over, the one named last changes fastest.
Arguments:
- prefill_query: bfloat16 [2, 1024, 8192], P('rep', 'ctx', 'head'), may hold values from -6 to 6
- prefill_key: bfloat16 [2, 1024, 8192], P('rep', 'ctx', 'head'), may hold values from -0.5390625 to 0.5390625
- prefill_value: bfloat16 [2, 1024, 8192], P('rep', 'ctx', 'head'), as said below
- prefill_rate: float32 [2, 64, 1024], P('rep', 'head', 'ctx'), as said below
- out_weight: bfloat16 [8192, 6144], P('head'), may hold values from -0.0625 to 0.0625
- decode_query: bfloat16 [256, 2, 8192], P(('ctx', 'rep'), None, 'head'), may hold values from -6 to 6
- decode_key: bfloat16 [256, 2, 8192], P(('ctx', 'rep'), None, 'head'), may hold values from -0.5390625 to 0.5390625
- decode_value: bfloat16 [256, 2, 8192], P(('ctx', 'rep'), None, 'head'), may hold values from -6 to 6
- decode_rate: float32 [256, 64, 2], P(('ctx', 'rep'), 'head'), may hold values from 0.01 to 0.5
- prompt_of_row: int32 [256], P(('ctx', 'rep')), may hold values from 0 to 1
Outputs:
- prefill_out: bfloat16 [2, 1024, 6144], P('rep', 'ctx', 'head')
- decode_out: bfloat16 [256, 2, 6144], P(('ctx', 'rep'), None, 'head')
The draws below stay inside these ranges and needn't reach their ends.
Inputs may be any that keep to these rules, and one draw needn't show every extreme that they name: `prefill_value`: values with row and column scales. `prefill_rate`: positive decay rates.
All inputs are finite; a program needn't handle non-finite values.
Results may differ from the reference program's by a relative error of at most 0.0055.
Values may be sent and summed in bfloat16 or wider, within the bound.
A program may use at most 64 MiB of HBM per device.

```python
import math
import jax
import jax.numpy as jnp
from jax import lax

D = 6144
HEAD_COUNT = 64
HEAD_DIM = 128
BLOCK = 256
TOK_DEV = 256
STEPS = 2
PROMPT_COUNT = 2
PROMPT_LENGTH = 1024
ROWS = 256
FEATURES = 8192


def draw_prefill_value(key, part):
    random_subkeys = jax.random.split(jax.random.fold_in(key, 11), 3)
    shape = (PROMPT_COUNT, PROMPT_LENGTH, FEATURES)
    baseline_level = jax.random.normal(random_subkeys[0], shape, jnp.float32)
    row_scale = jnp.exp(jax.random.uniform(random_subkeys[1], (PROMPT_COUNT, PROMPT_LENGTH, 1), jnp.float32, 0.0, math.log(10.0)))
    col_scale = jnp.exp(jax.random.uniform(random_subkeys[2], (1, 1, FEATURES), jnp.float32, 0.0, math.log(10.0)))
    return (0.1 * baseline_level * row_scale * col_scale).astype(jnp.bfloat16)


def draw_prefill_rate(key, part):
    random_subkeys = jax.random.split(jax.random.fold_in(key, 23), 7)
    fast_share = 0.5
    fast = jax.random.uniform(random_subkeys[0], (PROMPT_COUNT, HEAD_COUNT, 1), jnp.float32) < fast_share
    fast_rate = jnp.exp(jax.random.uniform(random_subkeys[1], (PROMPT_COUNT, HEAD_COUNT, 1), jnp.float32, math.log(1.0 / 50.0), math.log(1.0 / 20.0)))
    slow_rate = jnp.exp(jax.random.uniform(random_subkeys[2], (PROMPT_COUNT, HEAD_COUNT, 1), jnp.float32, math.log(0.05), math.log(0.3))) / PROMPT_LENGTH
    baseline_level = jnp.where(fast, fast_rate, slow_rate)
    groups = PROMPT_LENGTH // TOK_DEV
    group_multiplier = jnp.exp(jax.random.uniform(random_subkeys[3], (PROMPT_COUNT, HEAD_COUNT, groups), jnp.float32, math.log(0.5), math.log(2.0)))
    group_multiplier = jnp.repeat(group_multiplier, TOK_DEV, axis=2)
    jitter_amplitude = jax.random.uniform(random_subkeys[4], (PROMPT_COUNT, HEAD_COUNT, PROMPT_LENGTH), jnp.float32, 0.5, 1.5)
    spike_locations = jax.random.randint(random_subkeys[5], (PROMPT_COUNT, 2), 0, PROMPT_LENGTH)
    position_index = jnp.arange(PROMPT_LENGTH, dtype=jnp.int32)
    spike_selector = jnp.any(position_index[None, None, :] == spike_locations[:, :, None], axis=1)[:, None, :]
    spike_penalty = jax.random.uniform(random_subkeys[6], (PROMPT_COUNT, HEAD_COUNT, PROMPT_LENGTH), jnp.float32, 0.22, 0.6)
    decay_rate = baseline_level * group_multiplier * jitter_amplitude + jnp.where(spike_selector, spike_penalty, 0.0)
    return decay_rate.astype(jnp.float32)


def set_ends(values, key, least, top_value):
    dims = values.shape
    spot = [jax.random.randint(jax.random.fold_in(key, axis), (), 0, dims[axis]) for axis in range(len(dims))]
    values = values.at[tuple(spot)].set(least)
    longest = dims.index(max(dims))
    spot[longest] = (spot[longest] + 1) % dims[longest]
    return values.at[tuple(spot)].set(top_value)


def block_scale(stream_key, shape, cuts, low, high):
    def one(position, blocks):
        draws = jax.random.uniform(jax.random.fold_in(jax.random.fold_in(stream_key, 6), position), (blocks,), jnp.float32, low / len(cuts), high / len(cuts))
        return jnp.repeat(jnp.exp(draws), shape[position] // blocks).reshape((-1,) + (1,) * (len(shape) - position - 1))

    factor_of = one(*cuts[0])
    for cut in cuts[1:]:
        factor_of = factor_of * one(*cut)
    return factor_of


def normal_values(rng, shape, deviation, most, cuts=(), kind=jnp.bfloat16):
    values = jax.random.normal(rng, shape, jnp.float32) * deviation
    if len(cuts) > 0:
        values = block_scale(rng, shape, cuts, -0.22, 0.18) * values
    return jnp.clip(values, min=-most, max=most).astype(kind)


def setup_inputs(seed: int = 0) -> dict:
    seeds = jax.random.split(jax.random.key(seed), 11)
    prefill_query = normal_values(seeds[0], (PROMPT_COUNT, PROMPT_LENGTH, FEATURES), 1.0, 6.0, ((0, 2), (1, 4), (2, 32)))
    prefill_key = normal_values(seeds[1], (PROMPT_COUNT, PROMPT_LENGTH, FEATURES), 0.09, 0.5390625, ((0, 2), (1, 4), (2, 32)))
    prefill_value = draw_prefill_value(jax.random.fold_in(seeds[10], 71), 0)
    prefill_rate = draw_prefill_rate(jax.random.fold_in(seeds[10], 71), 0)
    out_weight = normal_values(seeds[4], (FEATURES, D), FEATURES ** -0.5, 0.0625, ((0, 32),))
    decode_query = normal_values(seeds[5], (ROWS, STEPS, FEATURES), 1.0, 6.0, ((0, 8), (2, 32)))
    decode_key = normal_values(seeds[6], (ROWS, STEPS, FEATURES), 0.09, 0.5390625, ((0, 8), (2, 32)))
    decode_value = normal_values(seeds[7], (ROWS, STEPS, FEATURES), 1.0, 6.0, ((0, 8), (2, 32)))
    decode_rate = jnp.clip(jnp.exp(math.log(0.5) - 3.912023 * jax.random.uniform(seeds[8], (ROWS, HEAD_COUNT, STEPS), jnp.float32) ** block_scale(seeds[8], (ROWS, HEAD_COUNT, STEPS), ((0, 8), (1, 32)), -0.2, 0.2)), 0.01, 0.5)
    prompt_of_row = set_ends(jax.random.randint(seeds[9], (ROWS,), 0, PROMPT_COUNT), jax.random.fold_in(seeds[9], 1), 0, PROMPT_COUNT - 1).astype(jnp.int32)
    return {"prefill_query": prefill_query, "prefill_key": prefill_key, "prefill_value": prefill_value, "prefill_rate": prefill_rate, "out_weight": out_weight, "decode_query": decode_query, "decode_key": decode_key, "decode_value": decode_value, "decode_rate": decode_rate, "prompt_of_row": prompt_of_row}


EPSILON = 1e-06
NEGATIVE = -1e+30
HIGH = lax.Precision.HIGHEST

def normalize(array):
    return array * lax.rsqrt(lax.optimization_barrier(jnp.mean(array * array, axis=-1, keepdims=True)) + EPSILON)

def reference(prefill_query, prefill_key, prefill_value, prefill_rate, out_weight, decode_query, decode_key, decode_value, decode_rate, prompt_of_row):
    prompts = prefill_query.shape[0]
    count = PROMPT_LENGTH // BLOCK

    def blocked(array):
        return array.reshape(prompts, count, BLOCK, HEAD_COUNT, HEAD_DIM).transpose(1, 0, 2, 3, 4)
    q_blocks = blocked(prefill_query)
    k_blocks = blocked(prefill_key)
    v_blocks = blocked(prefill_value)
    g_blocks = (-prefill_rate).reshape(prompts, HEAD_COUNT, count, BLOCK).transpose(2, 0, 1, 3)
    lower_mask = jnp.arange(BLOCK)[:, None] >= jnp.arange(BLOCK)[None, :]

    def advance(state, inputs):
        q_blk, k_blk, v_blk, g_blk = inputs
        q_f = q_blk.astype(jnp.float32)
        k_f = k_blk.astype(jnp.float32)
        v_f = v_blk.astype(jnp.float32)
        cumul = jnp.cumsum(g_blk, axis=-1)
        total = cumul[..., -1]
        decay = jnp.exp(jnp.where(lower_mask, cumul[..., :, None] - cumul[..., None, :], NEGATIVE))
        scores = jnp.einsum('pthd,pshd->phts', q_f, k_f)
        weights = (scores * decay).astype(jnp.bfloat16)
        weights = lax.optimization_barrier(weights).astype(jnp.float32)
        intra = jnp.einsum('phts,pshe->pthe', weights, v_f)
        inter = jnp.einsum('pthd,phde->pthe', q_f, state, precision=HIGH) * jnp.exp(cumul).transpose(0, 2, 1)[..., None]
        k_weighted = k_f * jnp.exp(total[..., None] - cumul).transpose(0, 2, 1)[..., None]
        new_state = jnp.exp(total)[..., None, None] * state + jnp.einsum('pshd,pshe->phde', k_weighted, v_f, precision=HIGH)
        return (new_state, intra + inter)
    start = jnp.zeros((prompts, HEAD_COUNT, HEAD_DIM, HEAD_DIM), jnp.float32)
    finals, outputs = lax.scan(advance, start, (q_blocks, k_blocks, v_blocks, g_blocks))
    attended = outputs.transpose(1, 0, 2, 3, 4).reshape(prompts, PROMPT_LENGTH, HEAD_COUNT, HEAD_DIM)
    hidden = normalize(attended).astype(jnp.bfloat16).reshape(prompts, PROMPT_LENGTH, HEAD_COUNT * HEAD_DIM)
    prefill_out = lax.map(lambda hidden_one: jnp.dot(hidden_one, out_weight, preferred_element_type=jnp.float32).astype(jnp.bfloat16), hidden)
    rows = decode_query.shape[0]

    def split_heads(array):
        return array.reshape(rows, STEPS, HEAD_COUNT, HEAD_DIM).astype(jnp.float32)
    d_query = split_heads(decode_query)
    d_key = split_heads(decode_key)
    d_value = split_heads(decode_value)
    cumul = jnp.cumsum(-decode_rate, axis=-1)
    onehot = (prompt_of_row[:, None] == jnp.arange(prompts, dtype=jnp.int32)[None, :]).astype(jnp.float32)
    start_terms = jnp.einsum('rthd,phde->prthe', d_query, finals, precision=HIGH)
    baseline_level = jnp.einsum('rp,prthe->rthe', onehot, start_terms, precision=HIGH) * jnp.exp(cumul).transpose(0, 2, 1)[..., None]
    step_mask = jnp.arange(STEPS)[:, None] >= jnp.arange(STEPS)[None, :]
    decay = jnp.exp(jnp.where(step_mask, cumul[..., :, None] - cumul[..., None, :], NEGATIVE))
    scores = jnp.einsum('rthd,rshd->rhts', d_query, d_key, precision=HIGH)
    intra = jnp.einsum('rhts,rshe->rthe', scores * decay, d_value, precision=HIGH)
    decode_hidden = normalize(baseline_level + intra).astype(jnp.bfloat16).reshape(rows * STEPS, HEAD_COUNT * HEAD_DIM)
    decode_out = jnp.dot(decode_hidden, out_weight, preferred_element_type=jnp.float32).astype(jnp.bfloat16).reshape(rows, STEPS, D)
    return (prefill_out, decode_out)
```

```python
import jax
import jax.numpy as jnp
from jax import lax
from jax.experimental import pallas as pl
from jax.experimental.pallas import tpu as pltpu
from jax.sharding import PartitionSpec as P

HD = 128
EPSILON = 1e-06
NEGATIVE = -1e30
HIGH = lax.Precision.HIGHEST
MESH = pl.DeviceIdType.MESH
F32 = jnp.float32
BF16 = jnp.bfloat16
OFFS = (2, 1, 3, 0)
ORDER = sorted(
    ((oy, ox) for oy in range(4) for ox in range(4)),
    key=lambda p: (max(p), p[0] + p[1], p[0]),
)
ROWS = 80
WIDE = 384
SROWS = 144


def dot(a, b, dims=((1,), (0,)), precision=None):
    return lax.dot_general(
        a, b, (dims, ((), ())), preferred_element_type=F32, precision=precision
    )


def split2(a):
    hi = a.astype(BF16)
    return hi, (a - hi.astype(F32)).astype(BF16)


def normalize(a):
    return a * lax.rsqrt(jnp.mean(a * a, axis=-1, keepdims=True) + EPSILON)


def kernel(
    q_hbm, k_hbm, v_hbm, g_hbm, w_hbm, dqkv_hbm, aux_hbm,
    out_ref, dec_ref,
    q_v, k_v, v_v, g_v, w_own, w_par, dqkv_v, aux_v,
    intra_v, bcol_v, dloc_v, st, hs, hr, s1, r1, own1, pk, ownf, r2, r2p,
    lsem, wsem, zs, zr, hsem, s1s, s1r, s2s, s2r, sps, spr,
):
    ctx = lax.axis_index("ctx")
    head = lax.axis_index("head")
    rep = lax.axis_index("rep")
    c = lax.rem(head, 2)
    x = lax.rem(lax.div(head, 2), 4)
    y = lax.div(head, 8)
    z = ctx * 2 + rep

    def dev(cc, xx, yy):
        return (ctx, (yy * 4 + xx) * 2 + cc, rep)

    def zdev(d):
        zz = lax.rem(z + d + 8, 8)
        return (lax.div(zz, 2), head, lax.rem(zz, 2))

    partner = dev(1 - c, x, y)

    def along(axis, d):
        return lax.rem((x if axis == 0 else y) + d, 4)

    def on_axis(axis, cc, d):
        if axis == 0:
            return dev(cc, lax.rem(x + d, 4), y)
        return dev(cc, x, lax.rem(y + d, 4))

    def rcopy(src, dst, ss, rs, device):
        return pltpu.make_async_remote_copy(
            src_ref=src, dst_ref=dst, send_sem=ss, recv_sem=rs,
            device_id=device, device_id_type=MESH,
        )

    loads = [
        pltpu.make_async_copy(a, b, lsem.at[i])
        for i, (a, b) in enumerate(
            ((g_hbm, g_v), (k_hbm, k_v), (v_hbm, v_v), (q_hbm, q_v),
             (dqkv_hbm, dqkv_v), (aux_hbm, aux_v), (w_hbm, w_own))
        )
    ]
    for cp in loads:
        cp.start()

    barrier = pltpu.get_barrier_semaphore()
    others = [partner, zdev(1), zdev(-1)]
    for axis in range(2):
        for d in (1, 2, 3):
            for cc in range(2):
                others.append(on_axis(axis, cc, d))
    for device in others:
        pl.semaphore_signal(barrier, inc=1, device_id=device, device_id_type=MESH)

    row = lax.broadcasted_iota(jnp.int32, (256, 256), 0)
    col = lax.broadcasted_iota(jnp.int32, (256, 256), 1)
    lower = (row >= col).astype(F32)
    upper = (row <= col).astype(F32)
    loads[0].wait()
    g = -g_v[...]
    brow = dot(g, upper, precision=HIGH)
    bcol = dot(lower, g, ((1,), (1,)), precision=HIGH)
    loads[1].wait()
    loads[2].wait()
    for h in range(2):
        hl = slice(HD * h, HD * h + HD)
        bc = bcol[:, h:h + 1]
        bcol_v[h] = jnp.broadcast_to(bc, (256, HD))
        total = brow[h:h + 1, 255:256]
        kw = k_v[:, hl].astype(F32) * jnp.exp(total - bc)
        khi, klo = split2(kw)
        vh = v_v[:, hl]
        own = dot(khi, vh, ((0,), (0,))) + dot(klo, vh, ((0,), (0,)))
        base = SROWS * h
        st[0, base:base + HD, :] = own.astype(BF16)
        l1 = total.astype(BF16)
        rem1 = total - l1.astype(F32)
        l2 = rem1.astype(BF16)
        l3 = (rem1 - l2.astype(F32)).astype(BF16)
        rows16 = lax.broadcasted_iota(jnp.int32, (16, HD), 0)
        logs = jnp.where(
            rows16 == 0, l1.astype(F32),
            jnp.where(rows16 == 1, l2.astype(F32), jnp.where(rows16 == 2, l3.astype(F32), 0.0)),
        )
        st[0, base + HD:base + SROWS, :] = logs.astype(BF16)

    pl.semaphore_wait(barrier, len(others))
    wcopy = rcopy(w_hbm, w_par, wsem.at[0], wsem.at[1], partner)
    wcopy.start()

    def zcopy(way, hop, h):
        rows = pl.ds(SROWS * h, SROWS)
        a = hop - 1 if way == 0 else (9 - hop) % 8
        b = hop if way == 0 else 8 - hop
        return rcopy(
            st.at[a, rows], st.at[b, rows], zs.at[way, hop - 1, h], zr.at[way, hop - 1, h],
            zdev(1 if way == 0 else -1),
        )

    def messages(hop):
        if hop < 4:
            return [(way, hop, h) for h in range(2) for way in range(2)]
        return [(0, 4, 0), (1, 4, 1)]

    for m in messages(1):
        zcopy(*m).start()

    def relay(hop):
        for way, _, h in messages(hop):
            zcopy(way, hop, h).wait_recv()
            if (way, hop + 1, h) in messages(hop + 1) if hop < 4 else False:
                zcopy(way, hop + 1, h).start()

    def local_part(h):
        hl = slice(HD * h, HD * h + HD)
        decay = jnp.exp(
            jnp.where(row >= col, bcol[:, h:h + 1] - brow[h:h + 1, :], NEGATIVE)
        )
        scores = dot(q_v[:, hl], k_v[:, hl], ((1,), (1,)))
        weights = (scores * decay).astype(BF16)
        intra_v[h] = dot(weights, v_v[:, hl])

    loads[3].wait()
    local_part(0)
    relay(1)
    local_part(1)
    relay(2)
    loads[4].wait()
    loads[5].wait()
    aux = aux_v[...]
    for h in range(2):
        hl = slice(HD * h, HD * h + HD)
        q0 = dqkv_v[0, :, hl].astype(F32)
        q1 = dqkv_v[1, :, hl].astype(F32)
        k0 = dqkv_v[2, :, hl].astype(F32)
        k1 = dqkv_v[3, :, hl].astype(F32)
        v0 = dqkv_v[4, :, hl].astype(F32)
        v1 = dqkv_v[5, :, hl].astype(F32)
        step1 = aux[:, 2 * h + 1:2 * h + 2]
        dloc_v[h, 0] = jnp.sum(q0 * k0, axis=-1, keepdims=True) * v0
        dloc_v[h, 1] = (
            jnp.sum(q1 * k0, axis=-1, keepdims=True) * jnp.exp(-step1) * v0
            + jnp.sum(q1 * k1, axis=-1, keepdims=True) * v1
        )
    relay(3)
    relay(4)

    def state(rel, h):
        base = SROWS * h
        s = st[rel, base:base + HD, :].astype(F32)
        logs = st[rel, base + HD:base + SROWS, :].astype(F32)
        return s, logs[0:1, :] + logs[1:2, :] + logs[2:3, :]

    def final_of(parts):
        total = None
        for m, (s, _) in enumerate(parts):
            cm = lax.rem(ctx - m + 4, 4)
            expo = jnp.zeros((1, HD), F32)
            for n, (_, ln) in enumerate(parts):
                if n != m:
                    cn = lax.rem(ctx - n + 4, 4)
                    expo = expo + jnp.where(cn > cm, ln, 0.0)
            term = jnp.exp(expo) * s
            total = term if total is None else total + term
        return total

    for h in range(2):
        hl = slice(HD * h, HD * h + HD)
        mine = [state(2 * m, h) for m in range(4)]
        other = [state(lax.rem(2 * m + 2 * rep + 7, 8), h) for m in range(4)]
        l1, l2 = mine[1][1], mine[2][1]
        entering = (
            jnp.where(ctx >= 1, 1.0, 0.0) * mine[1][0]
            + jnp.where(ctx >= 2, jnp.exp(l1), 0.0) * mine[2][0]
            + jnp.where(ctx >= 3, jnp.exp(l1 + l2), 0.0) * mine[3][0]
        )
        ehi, elo = split2(entering)
        qh = q_v[:, hl]
        attended = intra_v[h] + jnp.exp(bcol_v[h]) * (dot(qh, ehi) + dot(qh, elo))
        hid = normalize(attended).astype(BF16)
        for s in range(2):
            for axis in range(2):
                a = 128 * s + 64 * axis
                hs[s, ROWS * axis:ROWS * axis + 64, hl] = hid[a:a + 64]
        fin_mine = final_of(mine)
        fin_other = final_of(other)
        fin = (
            jnp.where(rep == 0, fin_mine, fin_other),
            jnp.where(rep == 0, fin_other, fin_mine),
        )
        d0 = aux[:, 2 * h:2 * h + 1]
        cums = (-d0, -d0 - aux[:, 2 * h + 1:2 * h + 2])
        second = aux[:, 4:5] > 0.5
        dq = dqkv_v[0:2, :, hl].reshape(64, HD)
        starts = []
        for p in range(2):
            fhi, flo = split2(fin[p])
            starts.append(dot(dq, fhi) + dot(dq, flo))
        for t in range(2):
            rows = slice(32 * t, 32 * t + 32)
            base = jnp.where(second, starts[1][rows], starts[0][rows])
            dh = normalize(base * jnp.exp(cums[t]) + dloc_v[h, t]).astype(BF16)
            for axis in range(2):
                r0 = ROWS * axis + 64
                hs[t, r0:r0 + 16, hl] = dh[16 * axis:16 * axis + 16]

    hcopy = rcopy(hs.at[1 - c], hr, hsem.at[0], hsem.at[1], partner)
    hcopy.start()
    loads[6].wait()
    wcopy.wait_recv()
    hcopy.wait_recv()

    def phase1(axis, oi, di):
        return rcopy(
            s1.at[axis, oi, di], r1.at[axis, oi, di], s1s.at[axis, oi, di], s1r.at[axis, oi, di],
            on_axis(axis, c, OFFS[di]),
        )

    mine_h = hs[c]
    part_h = hr[...]
    pending = []
    for iy, ix in ORDER:
        jy = lax.rem(y + OFFS[iy], 4)
        jx = lax.rem(x + OFFS[ix], 4)
        cols = pl.ds(pl.multiple_of((jy * 4 + jx) * WIDE, 128), WIDE)
        part = dot(mine_h, w_own[:, cols]) + dot(part_h, w_par[:, cols])
        ready = []
        for axis, (oi, di) in enumerate(((iy, ix), (ix, iy))):
            block = part[ROWS * axis:ROWS * axis + ROWS]
            if di == 3:
                own1[axis, oi] = block
            else:
                s1[axis, oi, di] = block.astype(BF16)
                ready.append((axis, oi, di))
        for m in pending:
            phase1(*m).start()
        pending = ready
    for m in pending:
        phase1(*m).start()

    lane = lax.broadcasted_iota(jnp.int32, (40, HD), 1)

    def phase2(axis, oi, part):
        return rcopy(
            pk.at[axis, oi, part], r2.at[axis, c, oi], s2s.at[axis, oi, part],
            s2r.at[axis, c, oi], on_axis(1 - axis, part, OFFS[oi]),
        )

    def phase2_own(axis):
        return rcopy(
            pk.at[axis, 3, 1 - c], r2p.at[axis], sps.at[axis], spr.at[axis], partner
        )

    pad = jnp.zeros((8, HD), F32)
    for oi in range(4):
        for axis in range(2):
            total = own1[axis, oi]
            for di in range(3):
                phase1(axis, oi, di).wait_recv()
                total = total + r1[axis, oi, di].astype(F32)
            t0, t1, t2 = (total[:, HD * i:HD * i + HD] for i in range(3))
            top, bottom = t1[0:40], t1[40:80]
            ea = jnp.where(lane < 64, top, pltpu.roll(bottom, 64, 1))
            eb = jnp.where(lane < 64, pltpu.roll(top, 64, 1), bottom)
            for part, (main, extra) in enumerate(((t0, ea), (t2, eb))):
                full = jnp.concatenate([main, extra, pad], axis=0)
                pk[axis, oi, part] = full.astype(BF16)
                if oi == 3:
                    ownf[axis, part] = full
        for axis in range(2):
            if oi < 3:
                for part in range(2):
                    phase2(axis, oi, part).start()
            else:
                phase2_own(axis).start()

    lane80 = lax.broadcasted_iota(jnp.int32, (ROWS, HD), 1)
    for axis in range(2):
        phase2_own(axis).wait_recv()
        for s in range(2):
            for oi in range(3):
                pltpu.make_async_remote_copy(
                    src_ref=pk.at[axis, oi, 0], dst_ref=r2.at[axis, s, oi],
                    send_sem=s2s.at[axis, oi, 0], recv_sem=s2r.at[axis, s, oi],
                    device_id=partner, device_id_type=MESH,
                ).wait_recv()
    for axis in range(2):
        for s in range(2):
            total = jnp.where(s == c, ownf[axis, c], r2p[axis].astype(F32))
            for oi in range(3):
                total = total + r2[axis, s, oi].astype(F32)
            main, extra = total[0:ROWS], total[ROWS:ROWS + 40]
            ext = jnp.concatenate([extra, pltpu.roll(extra, 64, 1)], axis=0)
            rolled = pltpu.roll(main, 64, 1)
            o0 = jnp.where(c == 0, main, jnp.where(lane80 < 64, ext, rolled)).astype(BF16)
            o1 = jnp.where(c == 0, ext, rolled).astype(BF16)
            a = 128 * s + 64 * axis
            out_ref[a:a + 64, 0:128] = o0[0:64]
            out_ref[a:a + 64, 128:192] = o1[0:64, 0:64]
            r = 16 * axis
            dec_ref[s, r:r + 16, 0:128] = o0[64:80]
            dec_ref[s, r:r + 16, 128:192] = o1[64:80, 0:64]

    wcopy.wait_send()
    hcopy.wait_send()
    for hop in range(1, 5):
        for m in messages(hop):
            zcopy(*m).wait_send()
    for axis in range(2):
        for oi in range(4):
            for di in range(3):
                phase1(axis, oi, di).wait_send()
        for oi in range(3):
            for part in range(2):
                phase2(axis, oi, part).wait_send()
        phase2_own(axis).wait_send()


def body(pq, pk_, pv, prate, w, dq, dk, dv, drate, prow):
    dqkv = jnp.stack([dq, dk, dv]).transpose(0, 2, 1, 3).reshape(6, 32, 256)
    aux = jnp.concatenate(
        [drate.reshape(32, 4), prow.astype(F32)[:, None], jnp.zeros((32, 3), F32)], axis=1
    )
    hbm = pl.BlockSpec(memory_space=pltpu.HBM)
    vmem = pl.BlockSpec(memory_space=pltpu.VMEM)
    dma = pltpu.SemaphoreType.DMA
    out, dec = pl.pallas_call(
        kernel,
        out_shape=(
            jax.ShapeDtypeStruct((256, 192), BF16),
            jax.ShapeDtypeStruct((2, 32, 192), BF16),
        ),
        in_specs=[hbm] * 7,
        out_specs=(vmem, vmem),
        scratch_shapes=[
            pltpu.VMEM((256, 256), BF16),
            pltpu.VMEM((256, 256), BF16),
            pltpu.VMEM((256, 256), BF16),
            pltpu.VMEM((2, 256), F32),
            pltpu.VMEM((256, 6144), BF16),
            pltpu.VMEM((256, 6144), BF16),
            pltpu.VMEM((6, 32, 256), BF16),
            pltpu.VMEM((32, 8), F32),
            pltpu.VMEM((2, 256, HD), F32),
            pltpu.VMEM((2, 256, HD), F32),
            pltpu.VMEM((2, 2, 32, HD), F32),
            pltpu.VMEM((8, 2 * SROWS, HD), BF16),
            pltpu.VMEM((2, 2 * ROWS, 256), BF16),
            pltpu.VMEM((2 * ROWS, 256), BF16),
            pltpu.VMEM((2, 4, 3, ROWS, WIDE), BF16),
            pltpu.VMEM((2, 4, 3, ROWS, WIDE), BF16),
            pltpu.VMEM((2, 4, ROWS, WIDE), F32),
            pltpu.VMEM((2, 4, 2, HD, HD), BF16),
            pltpu.VMEM((2, 2, HD, HD), F32),
            pltpu.VMEM((2, 2, 3, HD, HD), BF16),
            pltpu.VMEM((2, HD, HD), BF16),
            dma((7,)),
            dma((2,)),
            dma((2, 4, 2)),
            dma((2, 4, 2)),
            dma((2,)),
            dma((2, 4, 3)),
            dma((2, 4, 3)),
            dma((2, 3, 2)),
            dma((2, 2, 3)),
            dma((2,)),
            dma((2,)),
        ],
        compiler_params=pltpu.CompilerParams(
            collective_id=0, has_side_effects=True, vmem_limit_bytes=48 << 20
        ),
        name="lightning",
    )(pq[0], pk_[0], pv[0], prate[0], w, dqkv, aux)
    return out[None], dec.transpose(1, 0, 2)


def solution(mesh):
    return jax.shard_map(
        body,
        mesh=mesh,
        in_specs=(
            P("rep", "ctx", "head"),
            P("rep", "ctx", "head"),
            P("rep", "ctx", "head"),
            P("rep", "head", "ctx"),
            P("head", None),
            P(("ctx", "rep"), None, "head"),
            P(("ctx", "rep"), None, "head"),
            P(("ctx", "rep"), None, "head"),
            P(("ctx", "rep"), "head", None),
            P(("ctx", "rep")),
        ),
        out_specs=(P("rep", "ctx", "head"), P(("ctx", "rep"), None, "head")),
        check_vma=False,
    )
```

```python
import jax
import jax.numpy as jnp
from jax import lax
from jax.experimental import pallas as pl
from jax.experimental.pallas import tpu as pltpu
from jax.sharding import PartitionSpec as P

HD = 128
EPSILON = 1e-06
NEGATIVE = -1e30
HIGH = lax.Precision.HIGHEST
MESH = pl.DeviceIdType.MESH
F32 = jnp.float32
BF16 = jnp.bfloat16
OFFS = (2, 1, 3, 0)
FIRST = [(0, 0), (1, 0), (0, 1), (2, 0), (0, 2), (3, 0), (0, 3)]
ORDER = FIRST + [p for p in sorted(
    ((oy, ox) for oy in range(4) for ox in range(4)), key=lambda p: (max(p), p[0] + p[1], p[0])
) if p not in FIRST]
WIDE = 384
SROWS = 144


def dot(a, b, dims=((1,), (0,)), precision=None):
    return lax.dot_general(
        a, b, (dims, ((), ())), preferred_element_type=F32, precision=precision
    )


def split2(a):
    hi = a.astype(BF16)
    return hi, (a - hi.astype(F32)).astype(BF16)


def normalize(a):
    return a * lax.rsqrt(jnp.mean(a * a, axis=-1, keepdims=True) + EPSILON)


class Part:
    def __init__(self, rows, relay, refs):
        self.rows, self.relay = rows, relay
        (self.hs, self.hr, self.s1, self.r1, self.comb, self.own1, self.pk, self.ownf, self.r2, self.r2p,
         self.hsem, self.s1s, self.s1r, self.s2s, self.s2r, self.sps, self.spr) = refs

    @staticmethod
    def scratch(rows):
        dma = pltpu.SemaphoreType.DMA
        packed = -(-3 * rows // 2 // 16) * 16
        return [
            pltpu.VMEM((2, 2 * rows, 256), BF16),
            pltpu.VMEM((2 * rows, 256), BF16),
            pltpu.VMEM((2, 4, 3, rows, WIDE), BF16),
            pltpu.VMEM((2, 4, 3, rows, WIDE), BF16),
            pltpu.VMEM((2, 4, rows, WIDE), F32),
            pltpu.VMEM((2, 4, rows, WIDE), F32),
            pltpu.VMEM((2, 4, 2, packed, HD), BF16),
            pltpu.VMEM((2, 2, packed, HD), F32),
            pltpu.VMEM((2, 2, 3, packed, HD), BF16),
            pltpu.VMEM((2, packed, HD), BF16),
            dma((2,)),
            dma((2, 4, 3)), dma((2, 4, 3)),
            dma((2, 3, 2)), dma((2, 2, 3)),
            dma((2,)), dma((2,)),
        ]


def kernel(
    q_hbm, k_hbm, v_hbm, g_hbm, w_hbm, dq_hbm, dk_hbm, dv_hbm, dr_hbm, prow_hbm,
    out_ref, dec_ref,
    q_v, k_v, v_v, g_v, w_own, w_par, dqkv_v, dr_v, prow_v,
    intra_v, bcol_v, dloc_v, st, fs, fr,
    lsem, wss, wsr, zs, zr, z2s, z2r, fsem,
    *rest,
):
    pre = Part(64, True, rest[:len(rest) // 2])
    dec = Part(16, False, rest[len(rest) // 2:])
    ctx = lax.axis_index("ctx")
    head = lax.axis_index("head")
    rep = lax.axis_index("rep")
    c = lax.rem(head, 2)
    x = lax.rem(lax.div(head, 2), 4)
    y = lax.div(head, 8)

    def dev(cc, xx, yy):
        return (ctx, (yy * 4 + xx) * 2 + cc, rep)

    def cdev(d):
        return (lax.rem(ctx + d + 4, 4), head, rep)

    partner = dev(1 - c, x, y)
    twin = (ctx, head, 1 - rep)

    def on_axis(axis, cc, d):
        if axis == 0:
            return dev(cc, lax.rem(x + d, 4), y)
        return dev(cc, x, lax.rem(y + d, 4))

    def rcopy(src, dst, ss, rs, device):
        return pltpu.make_async_remote_copy(
            src_ref=src, dst_ref=dst, send_sem=ss, recv_sem=rs,
            device_id=device, device_id_type=MESH,
        )

    loads = [
        pltpu.make_async_copy(a, b, lsem.at[i])
        for i, (a, b) in enumerate(
            ((g_hbm, g_v), (k_hbm, k_v), (v_hbm, v_v), (q_hbm, q_v),
             (dq_hbm, dqkv_v.at[0]), (dk_hbm, dqkv_v.at[1]), (dv_hbm, dqkv_v.at[2]),
             (dr_hbm, dr_v), (prow_hbm, prow_v), (w_hbm, w_own))
        )
    ]
    for cp in loads:
        cp.start()

    barrier = pltpu.get_barrier_semaphore()
    others = [partner, twin, cdev(1), cdev(-1)]
    others += [on_axis(axis, cc, d) for axis in range(2) for d in (1, 2, 3) for cc in range(2)]
    for device in others:
        pl.semaphore_signal(barrier, inc=1, device_id=device, device_id_type=MESH)

    row = lax.broadcasted_iota(jnp.int32, (256, 256), 0)
    col = lax.broadcasted_iota(jnp.int32, (256, 256), 1)
    lower = (row >= col).astype(F32)
    upper = (row <= col).astype(F32)
    loads[0].wait()
    g = -g_v[...]
    brow = dot(g, upper, precision=HIGH)
    bcol = dot(lower, g, ((1,), (1,)), precision=HIGH)
    loads[1].wait()
    loads[2].wait()
    for h in range(2):
        hl = slice(HD * h, HD * h + HD)
        bc = bcol[:, h:h + 1]
        bcol_v[h] = jnp.broadcast_to(bc, (256, HD))
        total = brow[h:h + 1, 255:256]
        kw = k_v[:, hl].astype(F32) * jnp.exp(total - bc)
        khi, klo = split2(kw)
        vh = v_v[:, hl]
        own = dot(khi, vh, ((0,), (0,))) + dot(klo, vh, ((0,), (0,)))
        base = SROWS * h
        st[0, base:base + HD, :] = own.astype(BF16)
        l1 = total.astype(BF16)
        rem1 = total - l1.astype(F32)
        l2 = rem1.astype(BF16)
        l3 = (rem1 - l2.astype(F32)).astype(BF16)
        rows16 = lax.broadcasted_iota(jnp.int32, (16, HD), 0)
        logs = jnp.where(
            rows16 == 0, l1.astype(F32),
            jnp.where(rows16 == 1, l2.astype(F32), jnp.where(rows16 == 2, l3.astype(F32), 0.0)),
        )
        st[0, base + HD:base + SROWS, :] = logs.astype(BF16)

    pl.semaphore_wait(barrier, len(others))

    def zcopy(way, h):
        rows = pl.ds(SROWS * h, SROWS)
        return rcopy(
            st.at[0, rows], st.at[1 if way == 0 else 3, rows], zs.at[way, h], zr.at[way, h],
            cdev(1 if way == 0 else -1),
        )

    def zpass(way):
        rows = pl.ds(SROWS * way, SROWS)
        return rcopy(
            st.at[1 if way == 0 else 3, rows], st.at[2, rows], z2s.at[way], z2r.at[way],
            cdev(1 if way == 0 else -1),
        )

    def wcopy(i):
        rows = pl.ds(128 * i, 128)
        return rcopy(w_hbm.at[rows], w_par.at[rows], wss.at[i], wsr.at[i], partner)

    zcopy(0, 0).start()
    zcopy(1, 1).start()

    def local_part(h):
        hl = slice(HD * h, HD * h + HD)
        decay = jnp.exp(
            jnp.where(row >= col, bcol[:, h:h + 1] - brow[h:h + 1, :], NEGATIVE)
        )
        scores = dot(q_v[:, hl], k_v[:, hl], ((1,), (1,)))
        weights = (scores * decay).astype(BF16)
        intra_v[h] = dot(weights, v_v[:, hl])

    loads[3].wait()
    local_part(0)
    zcopy(0, 1).start()
    zcopy(1, 0).start()
    wcopy(0).start()
    local_part(1)
    for i in range(4, 9):
        loads[i].wait()
    pick = (
        lax.broadcasted_iota(jnp.int32, (64, 32), 0) // 2
        == lax.broadcasted_iota(jnp.int32, (64, 32), 1)
    ).astype(F32)
    odd = lax.rem(lax.broadcasted_iota(jnp.int32, (64, 1), 0), 2) == 1
    by_row = ((1,), (1,))
    second = dot(pick, jnp.broadcast_to(prow_v[...], (8, 32)).astype(F32), by_row)[:, 0:1] > 0.5
    dq2 = dqkv_v[0].reshape(64, 256)
    dk2 = dqkv_v[1].astype(F32).reshape(64, 256)
    dv2 = dqkv_v[2].astype(F32).reshape(64, 256)
    cums = []
    for h in range(2):
        hl = slice(HD * h, HD * h + HD)
        rates = dot(pick, dr_v[h], by_row, precision=HIGH)
        step1 = jnp.where(odd, rates[:, 1:2], 0.0)
        cums.append(-rates[:, 0:1] - step1)
        qf, kf, vf = dq2[:, hl].astype(F32), dk2[:, hl], dv2[:, hl]
        same = jnp.sum(qf * kf, axis=-1, keepdims=True)
        before = jnp.sum(qf * pltpu.roll(kf, 1, 0), axis=-1, keepdims=True)
        before = jnp.where(odd, before * jnp.exp(-step1), 0.0)
        dloc_v[h] = same * vf + before * pltpu.roll(vf, 1, 0)

    zcopy(0, 0).wait_recv()
    zpass(0).start()
    zcopy(1, 1).wait_recv()
    zpass(1).start()
    wcopy(1).start()
    zcopy(0, 1).wait_recv()
    zcopy(1, 0).wait_recv()
    zpass(0).wait_recv()
    zpass(1).wait_recv()

    def state(rel, h):
        base = SROWS * h
        s = st[rel, base:base + HD, :].astype(F32)
        logs = st[rel, base + HD:base + SROWS, :].astype(F32)
        return s, logs[0:1, :] + logs[1:2, :] + logs[2:3, :]

    for h in range(2):
        parts = [state(m, h) for m in range(4)]
        total = None
        for m, (s, _) in enumerate(parts):
            cm = lax.rem(ctx - m + 4, 4)
            expo = jnp.zeros((1, HD), F32)
            for n, (_, ln) in enumerate(parts):
                if n != m:
                    expo = expo + jnp.where(lax.rem(ctx - n + 4, 4) > cm, ln, 0.0)
            term = jnp.exp(expo) * s
            total = term if total is None else total + term
        fs[h] = total.astype(BF16)
    fcopy = rcopy(fs, fr, fsem.at[0], fsem.at[1], twin)
    for h in range(2):
        hl = slice(HD * h, HD * h + HD)
        (s1_, l1), (s2_, l2), (s3_, _) = (state(m, h) for m in (1, 2, 3))
        entering = (
            jnp.where(ctx >= 1, 1.0, 0.0) * s1_
            + jnp.where(ctx >= 2, jnp.exp(l1), 0.0) * s2_
            + jnp.where(ctx >= 3, jnp.exp(l1 + l2), 0.0) * s3_
        )
        ehi, elo = split2(entering)
        qh = q_v[:, hl]
        attended = intra_v[h] + jnp.exp(bcol_v[h]) * (dot(qh, ehi) + dot(qh, elo))
        hid = normalize(attended).astype(BF16)
        for s in range(2):
            pre.hs[s, :, hl] = hid[128 * s:128 * s + 128]

    def hcopy(part):
        return rcopy(part.hs.at[1 - c], part.hr, part.hsem.at[0], part.hsem.at[1], partner)

    fcopy.start()
    hcopy(pre).start()
    loads[9].wait()
    wcopy(0).wait_recv()
    wcopy(1).wait_recv()
    hcopy(pre).wait_recv()

    def phase1(part, axis, oi, di):
        d = OFFS[di]
        if part.relay and di == 0:
            d = 1 if oi % 2 == 0 else 3
        return rcopy(
            part.s1.at[axis, oi, di], part.r1.at[axis, oi, di],
            part.s1s.at[axis, oi, di], part.s1r.at[axis, oi, di], on_axis(axis, c, d),
        )

    def project(part):
        rows = part.rows
        mine_h = part.hs[c]
        part_h = part.hr[...]
        pending, held = [], []
        for n, (iy, ix) in enumerate(ORDER):
            jy = lax.rem(y + OFFS[iy], 4)
            jx = lax.rem(x + OFFS[ix], 4)
            cols = pl.ds(pl.multiple_of((jy * 4 + jx) * WIDE, 128), WIDE)
            both = dot(mine_h, w_own[:, cols]) + dot(part_h, w_par[:, cols])
            ready = []
            for axis, (oi, di) in enumerate(((iy, ix), (ix, iy))):
                block = both[rows * axis:rows * axis + rows]
                if di == 3:
                    part.own1[axis, oi] = block
                elif part.relay and di == 1 + oi % 2:
                    part.comb[axis, oi] = block
                else:
                    part.s1[axis, oi, di] = block.astype(BF16)
                    (ready if di == 0 else held).append((axis, oi, di))
            for m in pending:
                phase1(part, *m).start()
            pending = ready
            if n >= len(FIRST):
                pending, held = pending + held, []
        for m in pending:
            phase1(part, *m).start()

    def combine(part):
        pending = []
        for oi in range(4):
            di = 1 + oi % 2
            ready = []
            for axis in range(2):
                phase1(part, axis, oi, 0).wait_recv()
                both = part.comb[axis, oi] + part.r1[axis, oi, 0].astype(F32)
                part.s1[axis, oi, di] = both.astype(BF16)
                ready.append((axis, oi, di))
            for m in pending:
                phase1(part, *m).start()
            pending = ready
        for m in pending:
            phase1(part, *m).start()

    def phase2(part, axis, oi, p):
        return rcopy(
            part.pk.at[axis, oi, p], part.r2.at[axis, c, oi], part.s2s.at[axis, oi, p],
            part.s2r.at[axis, c, oi], on_axis(1 - axis, p, OFFS[oi]),
        )

    def phase2_own(part, axis):
        return rcopy(
            part.pk.at[axis, 3, 1 - c], part.r2p.at[axis], part.sps.at[axis], part.spr.at[axis],
            partner,
        )

    def scatter(part):
        rows, half = part.rows, part.rows // 2
        lane = lax.broadcasted_iota(jnp.int32, (half, HD), 1)
        extra_rows = part.pk.shape[3] - rows - half
        pending = []
        for oi in range(4):
            ready = []
            for axis in range(2):
                total = part.own1[axis, oi]
                for di in ((1, 2) if part.relay else (1, 2, 0)):
                    phase1(part, axis, oi, di).wait_recv()
                    total = total + part.r1[axis, oi, di].astype(F32)
                t0, t1, t2 = (total[:, HD * i:HD * i + HD] for i in range(3))
                top, bottom = t1[0:half], t1[half:rows]
                ea = jnp.where(lane < 64, top, pltpu.roll(bottom, 64, 1))
                eb = jnp.where(lane < 64, pltpu.roll(top, 64, 1), bottom)
                for p, (main, extra) in enumerate(((t0, ea), (t2, eb))):
                    full = [main, extra]
                    if extra_rows:
                        full.append(jnp.zeros((extra_rows, HD), F32))
                    full = jnp.concatenate(full, axis=0)
                    part.pk[axis, oi, p] = full.astype(BF16)
                    if oi == 3:
                        part.ownf[axis, p] = full
                if oi < 3:
                    ready += [phase2(part, axis, oi, p) for p in range(2)]
                else:
                    ready.append(phase2_own(part, axis))
                for copy in pending:
                    copy.start()
                pending, ready = ready, []
        for copy in pending:
            copy.start()

    def finish(part, store):
        rows, half = part.rows, part.rows // 2
        lane = lax.broadcasted_iota(jnp.int32, (rows, HD), 1)
        for axis in range(2):
            phase2_own(part, axis).wait_recv()
            for s in range(2):
                for oi in range(3):
                    rcopy(
                        part.pk.at[axis, oi, 0], part.r2.at[axis, s, oi],
                        part.s2s.at[axis, oi, 0], part.s2r.at[axis, s, oi], partner,
                    ).wait_recv()
        for axis in range(2):
            for s in range(2):
                total = jnp.where(s == c, part.ownf[axis, c], part.r2p[axis].astype(F32))
                for oi in range(3):
                    total = total + part.r2[axis, s, oi].astype(F32)
                main, extra = total[0:rows], total[rows:rows + half]
                ext = jnp.concatenate([extra, pltpu.roll(extra, 64, 1)], axis=0)
                rolled = pltpu.roll(main, 64, 1)
                o0 = jnp.where(c == 0, main, jnp.where(lane < 64, ext, rolled))
                o1 = jnp.where(c == 0, ext, rolled)
                store(rows * (2 * s + axis), o0.astype(BF16), o1.astype(BF16))

    project(pre)
    fcopy.wait_recv()
    for h in range(2):
        hl = slice(HD * h, HD * h + HD)
        fin = (
            dot(dq2[:, hl], fs[h]),
            dot(dq2[:, hl], fr[h]),
        )
        base = jnp.where(second == (rep == 1), fin[0], fin[1])
        dh = normalize(base * jnp.exp(cums[h]) + dloc_v[h]).astype(BF16)
        for s in range(2):
            dec.hs[s, :, hl] = dh[32 * s:32 * s + 32]
    hcopy(dec).start()
    combine(pre)
    hcopy(dec).wait_recv()
    project(dec)
    scatter(pre)
    scatter(dec)

    def store_pre(r, o0, o1):
        out_ref[r:r + 64, 0:128] = o0
        out_ref[r:r + 64, 128:192] = o1[:, 0:64]

    def store_dec(r, o0, o1):
        dec_ref[r:r + 16, 0:128] = o0
        dec_ref[r:r + 16, 128:192] = o1[:, 0:64]

    finish(pre, store_pre)
    finish(dec, store_dec)

    for i in range(2):
        wcopy(i).wait_send()
        zpass(i).wait_send()
        for h in range(2):
            zcopy(i, h).wait_send()
    fcopy.wait_send()
    for part in (pre, dec):
        hcopy(part).wait_send()
        for axis in range(2):
            for oi in range(4):
                for di in range(3):
                    phase1(part, axis, oi, di).wait_send()
            for p in range(2):
                for oi in range(3):
                    phase2(part, axis, oi, p).wait_send()
            phase2_own(part, axis).wait_send()


def body(pq, pk_, pv, prate, w, dq, dk, dv, drate, prow):
    hbm = pl.BlockSpec(memory_space=pltpu.HBM)
    vmem = pl.BlockSpec(memory_space=pltpu.VMEM)
    dma = pltpu.SemaphoreType.DMA
    out, dec = pl.pallas_call(
        kernel,
        out_shape=(
            pltpu.VMEM((256, 192), BF16),
            pltpu.VMEM((64, 192), BF16),
        ),
        in_specs=[hbm] * 10,
        out_specs=(vmem, vmem),
        scratch_shapes=[
            pltpu.VMEM((256, 256), BF16),
            pltpu.VMEM((256, 256), BF16),
            pltpu.VMEM((256, 256), BF16),
            pltpu.VMEM((2, 256), F32),
            pltpu.VMEM((256, 6144), BF16),
            pltpu.VMEM((256, 6144), BF16),
            pltpu.VMEM((3, 32, 2, 256), BF16),
            pltpu.VMEM((2, 2, 32), F32),
            pltpu.VMEM((1, 32), jnp.int32),
            pltpu.VMEM((2, 256, HD), F32),
            pltpu.VMEM((2, 256, HD), F32),
            pltpu.VMEM((2, 64, HD), F32),
            pltpu.VMEM((4, 2 * SROWS, HD), BF16),
            pltpu.VMEM((2, HD, HD), BF16),
            pltpu.VMEM((2, HD, HD), BF16),
            dma((10,)),
            dma((2,)),
            dma((2,)),
            dma((2, 2)),
            dma((2, 2)),
            dma((2,)),
            dma((2,)),
            dma((2,)),
            *Part.scratch(64),
            *Part.scratch(16),
        ],
        compiler_params=pltpu.CompilerParams(
            collective_id=0, has_side_effects=True, vmem_limit_bytes=48 << 20
        ),
        name="lightning",
    )(*(pltpu.with_memory_space_constraint(a, pltpu.HBM) for a in (
        pq[0], pk_[0], pv[0], prate[0], w, dq, dk, dv,
        drate.transpose(1, 2, 0), prow.reshape(1, 32),
    )))
    return out[None], dec.reshape(32, 2, 192)


def solution(mesh):
    return jax.shard_map(
        body,
        mesh=mesh,
        in_specs=(
            P("rep", "ctx", "head"),
            P("rep", "ctx", "head"),
            P("rep", "ctx", "head"),
            P("rep", "head", "ctx"),
            P("head", None),
            P(("ctx", "rep"), None, "head"),
            P(("ctx", "rep"), None, "head"),
            P(("ctx", "rep"), None, "head"),
            P(("ctx", "rep"), "head", None),
            P(("ctx", "rep")),
        ),
        out_specs=(P("rep", "ctx", "head"), P(("ctx", "rep"), None, "head")),
        check_vma=False,
    )
```

```python
import jax
import jax.numpy as jnp
from jax import lax
from jax.experimental import pallas as pl
from jax.experimental.pallas import tpu as pltpu
from jax.sharding import PartitionSpec as P

HD = 128
EPSILON = 1e-06
NEGATIVE = -1e30
HIGH = lax.Precision.HIGHEST
MESH = pl.DeviceIdType.MESH
F32 = jnp.float32
BF16 = jnp.bfloat16
OFFS = (2, 1, 3, 0)
FIRST = [(0, 0), (1, 0), (0, 1), (2, 0), (0, 2), (3, 0), (0, 3)]
ORDER = FIRST + [p for p in sorted(
    ((oy, ox) for oy in range(4) for ox in range(4)), key=lambda p: (max(p), p[0] + p[1], p[0])
) if p not in FIRST]
DORDER = FIRST + [(1, 1), (2, 1), (3, 1), (1, 2), (1, 3), (2, 2), (3, 2), (2, 3), (3, 3)]
WIDE = 384
BASE = (0, 144)
SIZE = (144, 128)


def dot(a, b, dims=((1,), (0,)), precision=None):
    return lax.dot_general(
        a, b, (dims, ((), ())), preferred_element_type=F32, precision=precision
    )


def split2(a):
    hi = a.astype(BF16)
    return hi, (a - hi.astype(F32)).astype(BF16)


def normalize(a):
    return a * lax.rsqrt(jnp.mean(a * a, axis=-1, keepdims=True) + EPSILON)


ROWS = 64
DROWS = 32
PACKED = 96


def packed(total):
    half = total.shape[0] // 2
    t0, t1, t2 = (total[:, HD * i:HD * i + HD] for i in range(3))
    top, bottom = t1[0:half], t1[half:]
    lane = lax.broadcasted_iota(jnp.int32, (half, HD), 1)
    ea = jnp.where(lane < 64, top, pltpu.roll(bottom, 64, 1))
    eb = jnp.where(lane < 64, pltpu.roll(top, 64, 1), bottom)
    return jnp.concatenate([t0, ea], axis=0), jnp.concatenate([t2, eb], axis=0)


def unpacked(total, c):
    rows = total.shape[0] * 2 // 3
    main, extra = total[0:rows], total[rows:]
    lane = lax.broadcasted_iota(jnp.int32, (rows, HD), 1)
    ext = jnp.concatenate([extra, pltpu.roll(extra, 64, 1)], axis=0)
    rolled = pltpu.roll(main, 64, 1)
    o0 = jnp.where(c == 0, main, jnp.where(lane < 64, ext, rolled))
    o1 = jnp.where(c == 0, ext, rolled)
    return o0.astype(BF16), o1[:, 0:64].astype(BF16)


def kernel(
    q_hbm, k_hbm, v_hbm, g_hbm, w_hbm, dq_hbm, dk_hbm, dv_hbm, dr_hbm, prow_hbm,
    out_ref, dec_ref,
    q_v, k_v, v_v, g_v, w_all, dqkv_v, dr_v, prow_v,
    intra_v, bcol_v, dloc_v, st, fs, fr,
    hb, acc, s1, rel, r1, comb, own1, pk, ownf, r2, dhs, dhr, d1s, d1r, dacc, down1, dpk, downf, d2r,
    lsem, wsem, zs, zr, fsem, hsem, dhsem, s1s, rels, r1s, psem, dsem,
):
    ctx = lax.axis_index("ctx")
    head = lax.axis_index("head")
    rep = lax.axis_index("rep")
    c = lax.rem(head, 2)
    x = lax.rem(lax.div(head, 2), 4)
    y = lax.div(head, 8)

    def dev(cc, xx, yy):
        return (ctx, (yy * 4 + xx) * 2 + cc, rep)

    def cdev(d):
        return (lax.rem(ctx + d + 4, 4), head, rep)

    partner = dev(1 - c, x, y)
    twin = (ctx, head, 1 - rep)

    def on_axis(axis, cc, d):
        if axis == 0:
            return dev(cc, lax.rem(x + d, 4), y)
        return dev(cc, x, lax.rem(y + d, 4))

    def rcopy(src, dst, ss, rs, device):
        return pltpu.make_async_remote_copy(
            src_ref=src, dst_ref=dst, send_sem=ss, recv_sem=rs,
            device_id=device, device_id_type=MESH,
        )

    loads = [
        pltpu.make_async_copy(a, b, lsem.at[i])
        for i, (a, b) in enumerate(
            ((g_hbm, g_v), (k_hbm, k_v), (v_hbm, v_v), (q_hbm, q_v),
             (dq_hbm, dqkv_v.at[0]), (dk_hbm, dqkv_v.at[1]), (dv_hbm, dqkv_v.at[2]),
             (dr_hbm, dr_v), (prow_hbm, prow_v), (w_hbm, w_all.at[0]))
        )
    ]
    for cp in loads:
        cp.start()

    barrier = pltpu.get_barrier_semaphore()
    others = [partner, twin, cdev(1), cdev(3)]
    others += [on_axis(axis, cc, d) for axis in range(2) for d in (1, 2, 3) for cc in range(2)]
    for device in others:
        pl.semaphore_signal(barrier, inc=1, device_id=device, device_id_type=MESH)

    row = lax.broadcasted_iota(jnp.int32, (256, 256), 0)
    col = lax.broadcasted_iota(jnp.int32, (256, 256), 1)
    lower = (row >= col).astype(F32)
    upper = (row <= col).astype(F32)
    loads[0].wait()
    g = -g_v[...]
    brow = dot(g, upper, precision=HIGH)
    bcol = dot(lower, g, ((1,), (1,)), precision=HIGH)
    loads[1].wait()
    loads[2].wait()
    rows16 = lax.broadcasted_iota(jnp.int32, (16, HD), 0)
    logs = jnp.zeros((16, HD), F32)
    for h in range(2):
        hl = slice(HD * h, HD * h + HD)
        bc = bcol[:, h:h + 1]
        bcol_v[h] = jnp.broadcast_to(bc, (256, HD))
        total = brow[h:h + 1, 255:256]
        kw = k_v[:, hl].astype(F32) * jnp.exp(total - bc)
        khi, klo = split2(kw)
        vh = v_v[:, hl]
        own = dot(khi, vh, ((0,), (0,))) + dot(klo, vh, ((0,), (0,)))
        st[0, BASE[h]:BASE[h] + HD, :] = own.astype(BF16)
        l1 = total.astype(BF16).astype(F32)
        l2 = (total - l1).astype(BF16).astype(F32)
        for i, term in enumerate((l1, l2, total - l1 - l2)):
            logs = jnp.where(rows16 == 3 * h + i, term, logs)
    st[0, HD:HD + 16, :] = logs.astype(BF16)

    pl.semaphore_wait(barrier, len(others))

    def zcopy(way, h):
        rows = pl.ds(BASE[h], SIZE[h])
        return rcopy(
            st.at[0, rows], st.at[1 + 2 * way, rows], zs.at[way], zr.at[way, h], cdev(1 + 2 * way)
        )

    def zpass(way):
        rows = pl.ds(BASE[way], SIZE[way])
        return rcopy(
            st.at[1 + 2 * way, rows], st.at[2, rows], zs.at[2], zr.at[2, way], cdev(1 + 2 * way)
        )

    wcopy = rcopy(w_hbm, w_all.at[1], wsem.at[0], wsem.at[1], partner)

    zcopy(0, 0).start()
    zcopy(1, 1).start()
    wcopy.start()

    def local_part(h):
        hl = slice(HD * h, HD * h + HD)
        decay = jnp.exp(
            jnp.where(row >= col, bcol[:, h:h + 1] - brow[h:h + 1, :], NEGATIVE)
        )
        scores = dot(q_v[:, hl], k_v[:, hl], ((1,), (1,)))
        weights = (scores * decay).astype(BF16)
        intra_v[h] = dot(weights, v_v[:, hl])

    loads[3].wait()
    local_part(0)
    zcopy(0, 1).start()
    zcopy(1, 0).start()
    local_part(1)
    for i in range(4, 9):
        loads[i].wait()
    pick = (
        lax.broadcasted_iota(jnp.int32, (64, 32), 0) // 2
        == lax.broadcasted_iota(jnp.int32, (64, 32), 1)
    ).astype(F32)
    odd = lax.rem(lax.broadcasted_iota(jnp.int32, (64, 1), 0), 2) == 1
    by_row = ((1,), (1,))
    second = dot(pick, jnp.broadcast_to(prow_v[...], (8, 32)).astype(F32), by_row)[:, 0:1] > 0.5
    dq2 = dqkv_v[0].reshape(64, 256)
    dk2 = dqkv_v[1].astype(F32).reshape(64, 256)
    dv2 = dqkv_v[2].astype(F32).reshape(64, 256)
    cums = []
    for h in range(2):
        hl = slice(HD * h, HD * h + HD)
        rates = dot(pick, dr_v[h], by_row, precision=HIGH)
        step1 = jnp.where(odd, rates[:, 1:2], 0.0)
        cums.append(-rates[:, 0:1] - step1)
        qf, kf, vf = dq2[:, hl].astype(F32), dk2[:, hl], dv2[:, hl]
        same = jnp.sum(qf * kf, axis=-1, keepdims=True)
        before = jnp.sum(qf * pltpu.roll(kf, 1, 0), axis=-1, keepdims=True)
        before = jnp.where(odd, before * jnp.exp(-step1), 0.0)
        dloc_v[h] = same * vf + before * pltpu.roll(vf, 1, 0)

    for way in range(2):
        zcopy(way, way).wait_recv()
        zpass(way).start()
    def state(rel, h):
        s = st[rel, BASE[h]:BASE[h] + HD, :].astype(F32)
        logs = st[rel, HD:HD + 16, :].astype(F32)
        i = 3 * h
        return s, logs[i:i + 1, :] + logs[i + 1:i + 2, :] + logs[i + 2:i + 3, :]

    fcopy = rcopy(fs, fr, fsem.at[0], fsem.at[1], twin)
    hcopy = rcopy(hb.at[1 - c], hb.at[2], hsem.at[0], hsem.at[1], partner)
    dhcopy = rcopy(dhs.at[1 - c], dhr, dhsem.at[0], dhsem.at[1], partner)

    def hidden():
        for way in range(2):
            zcopy(way, 1 - way).wait_recv()
        for way in range(2):
            zpass(way).wait_recv()
        for h in range(2):
            parts = [state(m, h) for m in range(4)]
            total = None
            for m, (s, _) in enumerate(parts):
                cm = lax.rem(ctx - m + 4, 4)
                expo = jnp.zeros((1, HD), F32)
                for n, (_, ln) in enumerate(parts):
                    if n != m:
                        expo = expo + jnp.where(lax.rem(ctx - n + 4, 4) > cm, ln, 0.0)
                term = jnp.exp(expo) * s
                total = term if total is None else total + term
            fs[h] = total.astype(BF16)
        for h in range(2):
            hl = slice(HD * h, HD * h + HD)
            (s1_, l1), (s2_, l2), (s3_, _) = (state(m, h) for m in (1, 2, 3))
            entering = (
                jnp.where(ctx >= 1, 1.0, 0.0) * s1_
                + jnp.where(ctx >= 2, jnp.exp(l1), 0.0) * s2_
                + jnp.where(ctx >= 3, jnp.exp(l1 + l2), 0.0) * s3_
            )
            ehi, elo = split2(entering)
            qh = q_v[:, hl]
            attended = intra_v[h] + jnp.exp(bcol_v[h]) * (dot(qh, ehi) + dot(qh, elo))
            hid = normalize(attended).astype(BF16)
            for s in range(2):
                hb[s, :, hl] = hid[128 * s:128 * s + 128]
            if h == 0:
                fcopy.start()
        hcopy.start()

    def columns(oy, ox):
        jy = lax.rem(y + oy, 4)
        jx = lax.rem(x + ox, 4)
        return pl.ds(pl.multiple_of((jy * 4 + jx) * WIDE, 128), WIDE)

    pl.when(c == 1)(hidden)
    pl.when(c == 0)(hcopy.wait_recv)
    loads[9].wait()
    wcopy.wait_recv()
    first = hb[2 - c]
    for n, (iy, ix) in enumerate(ORDER):
        acc[n] = dot(first, w_all[1 - c, :, columns(OFFS[iy], OFFS[ix])])
    pl.when(c == 0)(hidden)
    pl.when(c == 1)(hcopy.wait_recv)

    def phase1(axis, oi, di):
        if di == 0:
            return rcopy(
                s1.at[axis, oi, 0], rel.at[oi, axis], s1s.at[0], rels.at[oi],
                on_axis(axis, c, 1 if oi % 2 == 0 else 3),
            )
        return rcopy(
            s1.at[axis, oi, di], r1.at[oi, axis, di - 1], s1s.at[0], r1s.at[oi],
            on_axis(axis, c, OFFS[di]),
        )

    later = []

    def flush(new=()):
        for copy in later:
            copy.start()
        later[:] = new

    def project():
        second_h = hb[2 * c]
        held = []
        for n, (iy, ix) in enumerate(ORDER):
            both = acc[n] + dot(second_h, w_all[c, :, columns(OFFS[iy], OFFS[ix])])
            ready = []
            for axis, (oi, di) in enumerate(((iy, ix), (ix, iy))):
                block = both[ROWS * axis:ROWS * axis + ROWS]
                if di == 3:
                    own1[axis, oi] = block
                elif di == 1 + oi % 2:
                    comb[axis, oi] = block
                else:
                    s1[axis, oi, di] = block.astype(BF16)
                    (ready if di == 0 else held).append(phase1(axis, oi, di))
            if n >= len(FIRST):
                ready, held = ready + held, []
            flush(ready)

    def combine(oi):
        di = 1 + oi % 2
        rcopy(s1.at[0, 0:2, 0], rel.at[oi], s1s.at[0], rels.at[oi], partner).wait_recv()
        ready = []
        for axis in range(2):
            both = comb[axis, oi] + rel[oi, axis].astype(F32)
            s1[axis, oi, di] = both.astype(BF16)
            ready.append(phase1(axis, oi, di))
        flush(ready)

    def decode_own(between):
        mine_h = dhs[c]
        for n, (iy, ix) in enumerate(DORDER):
            dacc[n] = dot(mine_h, w_all[0, :, columns(OFFS[iy], OFFS[ix])])
            if n in between:
                between[n]()

    def decode_first(axis, di):
        return rcopy(
            d1s.at[axis, di], d1r.at[axis, di], dsem.at[0], dsem.at[1], on_axis(axis, c, OFFS[di])
        )

    def decode_rest(between):
        part_h = dhr[...]
        left = {(axis, di): 4 for axis in range(2) for di in range(3)}
        for n, (iy, ix) in enumerate(DORDER):
            both = dacc[n] + dot(part_h, w_all[1, :, columns(OFFS[iy], OFFS[ix])])
            ready = []
            for axis, (oi, di) in enumerate(((iy, ix), (ix, iy))):
                block = both[16 * axis:16 * axis + 16]
                if di == 3:
                    down1[axis, oi] = block
                else:
                    d1s[axis, di, oi] = block.astype(BF16)
                    left[axis, di] -= 1
                    if left[axis, di] == 0:
                        ready.append(decode_first(axis, di))
            flush(ready)
            if n in between:
                between[n]()

    def phase2(axis, oi, p):
        return rcopy(
            pk.at[(axis * 3 + oi) * 2 + p], r2.at[(axis * 3 + oi) * 2 + c], psem.at[0], psem.at[1],
            on_axis(1 - axis, p, OFFS[oi]),
        )

    def scatter(oi):
        rcopy(s1.at[:, 0:2, 0], r1.at[oi], s1s.at[0], r1s.at[oi], partner).wait_recv()
        for axis in range(2):
            total = own1[axis, oi] + r1[oi, axis, 0].astype(F32) + r1[oi, axis, 1].astype(F32)
            pa, pb = packed(total)
            if oi < 3:
                slot = (axis * 3 + oi) * 2
                pk[slot] = pa.astype(BF16)
                pk[slot + 1] = pb.astype(BF16)
                flush([phase2(axis, oi, p) for p in range(2)])
            else:
                ownf[axis] = jnp.where(c == 0, pa, pb)
                pk[12 + axis] = jnp.where(c == 0, pb, pa).astype(BF16)
                flush([rcopy(
                    pk.at[12 + axis], r2.at[12 + axis], psem.at[0], psem.at[1], partner
                )])

    def decode_scatter():
        all_first = rcopy(d1s, d1r, dsem.at[0], dsem.at[1], partner)
        all_first.wait_recv()
        pad = jnp.zeros((8, HD), F32)
        for oi in range(4):
            for axis in range(2):
                total = down1[axis, oi]
                for di in range(3):
                    total = total + d1r[axis, di, oi].astype(F32)
                pa, pb = (jnp.concatenate([p, pad], axis=0) for p in packed(total))
                if oi < 3:
                    slot = (axis * 3 + oi) * 2
                    dpk[slot] = pa.astype(BF16)
                    dpk[slot + 1] = pb.astype(BF16)
                    flush([
                        rcopy(
                            dpk.at[slot + p], d2r.at[slot + c], dsem.at[2], dsem.at[3],
                            on_axis(1 - axis, p, OFFS[oi]),
                        )
                        for p in range(2)
                    ])
                else:
                    downf[axis] = jnp.where(c == 0, pa, pb)
                    dpk[12 + axis] = jnp.where(c == 0, pb, pa).astype(BF16)
                    flush([rcopy(
                        dpk.at[12 + axis], d2r.at[12 + axis], dsem.at[2], dsem.at[3], partner
                    )])

    project()
    fcopy.wait_recv()
    for h in range(2):
        hl = slice(HD * h, HD * h + HD)
        fin = (
            dot(dq2[:, hl], fs[h]),
            dot(dq2[:, hl], fr[h]),
        )
        base = jnp.where(second == (rep == 1), fin[0], fin[1])
        dh = normalize(base * jnp.exp(cums[h]) + dloc_v[h]).astype(BF16)
        for s in range(2):
            dhs[s, :, hl] = dh[32 * s:32 * s + 32]
    flush([dhcopy])
    combine(0)
    decode_own({7: lambda: combine(1), 15: lambda: combine(2)})
    dhcopy.wait_recv()
    decode_rest({2: lambda: combine(3)})
    for oi in range(3):
        scatter(oi)
    decode_scatter()
    scatter(3)
    flush()
    all_pre = rcopy(pk, r2, psem.at[0], psem.at[1], partner)
    all_pre.wait_recv()
    for axis in range(2):
        for s in range(2):
            total = jnp.where(s == c, ownf[axis], r2[12 + axis].astype(F32))
            for oi in range(3):
                total = total + r2[(axis * 3 + oi) * 2 + s].astype(F32)
            o0, o1 = unpacked(total, c)
            r = ROWS * (2 * s + axis)
            out_ref[r:r + ROWS, 0:128] = o0
            out_ref[r:r + ROWS, 128:192] = o1

    all_dec = rcopy(dpk, d2r, dsem.at[2], dsem.at[3], partner)
    all_dec.wait_recv()
    for axis in range(2):
        for s in range(2):
            total = jnp.where(s == c, downf[axis], d2r[12 + axis].astype(F32))
            for oi in range(3):
                total = total + d2r[(axis * 3 + oi) * 2 + s].astype(F32)
            o0, o1 = unpacked(total[0:24], c)
            r = 16 * (2 * s + axis)
            dec_ref[r:r + 16, 0:128] = o0
            dec_ref[r:r + 16, 128:192] = o1

    wcopy.wait_send()
    for i in range(3):
        rcopy(st.at[0], st.at[2], zs.at[i], zr.at[0, 0], partner).wait_send()
    fcopy.wait_send()
    hcopy.wait_send()
    dhcopy.wait_send()
    rcopy(s1, s1, s1s.at[0], r1s.at[0], partner).wait_send()
    rcopy(d1s, d1r, dsem.at[0], dsem.at[1], partner).wait_send()
    all_dec.wait_send()
    all_pre.wait_send()


def body(pq, pk_, pv, prate, w, dq, dk, dv, drate, prow):
    hbm = pl.BlockSpec(memory_space=pltpu.HBM)
    vmem = pl.BlockSpec(memory_space=pltpu.VMEM)
    dma = pltpu.SemaphoreType.DMA
    out, dec = pl.pallas_call(
        kernel,
        out_shape=(
            pltpu.VMEM((256, 192), BF16),
            pltpu.VMEM((64, 192), BF16),
        ),
        in_specs=[hbm] * 10,
        out_specs=(vmem, vmem),
        scratch_shapes=[
            pltpu.VMEM((256, 256), BF16),
            pltpu.VMEM((256, 256), BF16),
            pltpu.VMEM((256, 256), BF16),
            pltpu.VMEM((2, 256), F32),
            pltpu.VMEM((2, 256, 6144), BF16),
            pltpu.VMEM((3, 32, 2, 256), BF16),
            pltpu.VMEM((2, 2, 32), F32),
            pltpu.VMEM((1, 32), jnp.int32),
            pltpu.VMEM((2, 256, HD), F32),
            pltpu.VMEM((2, 256, HD), F32),
            pltpu.VMEM((2, 64, HD), F32),
            pltpu.VMEM((4, 2 * HD + 16, HD), BF16),
            pltpu.VMEM((2, HD, HD), BF16),
            pltpu.VMEM((2, HD, HD), BF16),
            pltpu.VMEM((3, 2 * ROWS, 256), BF16),
            pltpu.VMEM((16, 2 * ROWS, WIDE), F32),
            pltpu.VMEM((2, 4, 3, ROWS, WIDE), BF16),
            pltpu.VMEM((4, 2, ROWS, WIDE), BF16),
            pltpu.VMEM((4, 2, 2, ROWS, WIDE), BF16),
            pltpu.VMEM((2, 4, ROWS, WIDE), F32),
            pltpu.VMEM((2, 4, ROWS, WIDE), F32),
            pltpu.VMEM((14, PACKED, HD), BF16),
            pltpu.VMEM((2, PACKED, HD), F32),
            pltpu.VMEM((14, PACKED, HD), BF16),
            pltpu.VMEM((2, DROWS, 256), BF16),
            pltpu.VMEM((DROWS, 256), BF16),
            pltpu.VMEM((2, 3, 4, 16, WIDE), BF16),
            pltpu.VMEM((2, 3, 4, 16, WIDE), BF16),
            pltpu.VMEM((16, DROWS, WIDE), F32),
            pltpu.VMEM((2, 4, 16, WIDE), F32),
            pltpu.VMEM((14, 32, HD), BF16),
            pltpu.VMEM((2, 32, HD), F32),
            pltpu.VMEM((14, 32, HD), BF16),
            dma((10,)),
            dma((2,)),
            dma((3,)),
            dma((3, 2)),
            dma((2,)),
            dma((2,)),
            dma((2,)),
            dma((1,)),
            dma((4,)),
            dma((4,)),
            dma((2,)),
            dma((4,)),
        ],
        compiler_params=pltpu.CompilerParams(
            collective_id=0, has_side_effects=True, vmem_limit_bytes=48 << 20
        ),
        name="lightning",
    )(*(pltpu.with_memory_space_constraint(a, pltpu.HBM) for a in (
        pq[0], pk_[0], pv[0], prate[0], w, dq, dk, dv,
        drate.transpose(1, 2, 0), prow.reshape(1, 32),
    )))
    return out[None], dec.reshape(32, 2, 192)


def solution(mesh):
    return jax.shard_map(
        body,
        mesh=mesh,
        in_specs=(
            P("rep", "ctx", "head"),
            P("rep", "ctx", "head"),
            P("rep", "ctx", "head"),
            P("rep", "head", "ctx"),
            P("head", None),
            P(("ctx", "rep"), None, "head"),
            P(("ctx", "rep"), None, "head"),
            P(("ctx", "rep"), None, "head"),
            P(("ctx", "rep"), "head", None),
            P(("ctx", "rep")),
        ),
        out_specs=(P("rep", "ctx", "head"), P(("ctx", "rep"), None, "head")),
        check_vma=False,
    )
```

```python
import jax
import jax.numpy as jnp
from jax import lax
from jax.experimental import pallas as pl
from jax.experimental.pallas import tpu as pltpu
from jax.sharding import PartitionSpec as P

HD = 128
EPSILON = 1e-06
NEGATIVE = -1e30
HIGH = lax.Precision.HIGHEST
MESH = pl.DeviceIdType.MESH
F32 = jnp.float32
BF16 = jnp.bfloat16
OFFS = (2, 1, 3, 0)
FIRST = [(0, 0), (1, 0), (0, 1), (2, 0), (0, 2), (3, 0), (0, 3)]
ORDER = FIRST + [p for p in sorted(
    ((oy, ox) for oy in range(4) for ox in range(4)), key=lambda p: (max(p), p[0] + p[1], p[0])
) if p not in FIRST]
DORDER = FIRST + [(1, 1), (2, 1), (3, 1), (1, 2), (1, 3), (2, 2), (3, 2), (2, 3), (3, 3)]
WIDE = 384
BASE = (0, 144)
SIZE = (144, 128)


def dot(a, b, dims=((1,), (0,)), precision=None):
    return lax.dot_general(
        a, b, (dims, ((), ())), preferred_element_type=F32, precision=precision
    )


def split2(a):
    hi = a.astype(BF16)
    return hi, (a - hi.astype(F32)).astype(BF16)


def normalize(a):
    return a * lax.rsqrt(jnp.mean(a * a, axis=-1, keepdims=True) + EPSILON)


ROWS = 64
DROWS = 32
PACKED = 96


def packed(total):
    half = total.shape[0] // 2
    t0, t1, t2 = (total[:, HD * i:HD * i + HD] for i in range(3))
    top, bottom = t1[0:half], t1[half:]
    lane = lax.broadcasted_iota(jnp.int32, (half, HD), 1)
    ea = jnp.where(lane < 64, top, pltpu.roll(bottom, 64, 1))
    eb = jnp.where(lane < 64, pltpu.roll(top, 64, 1), bottom)
    return jnp.concatenate([t0, ea], axis=0), jnp.concatenate([t2, eb], axis=0)


def unpacked(total, c):
    rows = total.shape[0] * 2 // 3
    main, extra = total[0:rows], total[rows:]
    lane = lax.broadcasted_iota(jnp.int32, (rows, HD), 1)
    ext = jnp.concatenate([extra, pltpu.roll(extra, 64, 1)], axis=0)
    rolled = pltpu.roll(main, 64, 1)
    o0 = jnp.where(c == 0, main, jnp.where(lane < 64, ext, rolled))
    o1 = jnp.where(c == 0, ext, rolled)
    return o0.astype(BF16), o1[:, 0:64].astype(BF16)


def kernel(
    q_hbm, k_hbm, v_hbm, g_hbm, w_hbm, dq_hbm, dk_hbm, dv_hbm, dr_hbm, prow_hbm,
    out_ref, dec_ref,
    q_v, k_v, v_v, g_v, w_all, dqkv_v, dr_v, prow_v,
    intra_v, bcol_v, dloc_v, st, fs, fr,
    hb, acc, s1, rel, r1, comb, own1, pk, ownf, r2, dhs, dhr, d1s, d1r, dacc, down1, dpk, downf, d2r,
    lsem, wsem, zs, zr, fsem, hsem, dhsem, s1s, rels, r1s, psem, dsem,
):
    ctx = lax.axis_index("ctx")
    head = lax.axis_index("head")
    rep = lax.axis_index("rep")
    c = lax.rem(head, 2)
    x = lax.rem(lax.div(head, 2), 4)
    y = lax.div(head, 8)

    def dev(cc, xx, yy):
        return (ctx, (yy * 4 + xx) * 2 + cc, rep)

    def cdev(d):
        return (lax.rem(ctx + d + 4, 4), head, rep)

    partner = dev(1 - c, x, y)
    twin = (ctx, head, 1 - rep)

    def on_axis(axis, cc, d):
        if axis == 0:
            return dev(cc, lax.rem(x + d, 4), y)
        return dev(cc, x, lax.rem(y + d, 4))

    def rcopy(src, dst, ss, rs, device):
        return pltpu.make_async_remote_copy(
            src_ref=src, dst_ref=dst, send_sem=ss, recv_sem=rs,
            device_id=device, device_id_type=MESH,
        )

    loads = [
        pltpu.make_async_copy(a, b, lsem.at[i])
        for i, (a, b) in enumerate(
            ((g_hbm, g_v), (k_hbm, k_v), (v_hbm, v_v), (q_hbm, q_v),
             (dq_hbm, dqkv_v.at[0]), (dk_hbm, dqkv_v.at[1]), (dv_hbm, dqkv_v.at[2]),
             (dr_hbm, dr_v), (prow_hbm, prow_v), (w_hbm, w_all.at[0]))
        )
    ]
    for cp in loads:
        cp.start()

    barrier = pltpu.get_barrier_semaphore()
    others = [partner, twin, cdev(1), cdev(3)]
    others += [on_axis(axis, cc, d) for axis in range(2) for d in (1, 2, 3) for cc in range(2)]
    for device in others:
        pl.semaphore_signal(barrier, inc=1, device_id=device, device_id_type=MESH)

    row = lax.broadcasted_iota(jnp.int32, (256, 256), 0)
    col = lax.broadcasted_iota(jnp.int32, (256, 256), 1)
    lower = (row >= col).astype(F32)
    upper = (row <= col).astype(F32)
    loads[0].wait()
    g = -g_v[...]
    brow = dot(g, upper, precision=HIGH)
    bcol = dot(lower, g, ((1,), (1,)), precision=HIGH)
    loads[1].wait()
    loads[2].wait()
    rows16 = lax.broadcasted_iota(jnp.int32, (16, HD), 0)
    logs = jnp.zeros((16, HD), F32)
    for h in range(2):
        hl = slice(HD * h, HD * h + HD)
        bc = bcol[:, h:h + 1]
        bcol_v[h] = jnp.broadcast_to(bc, (256, HD))
        total = brow[h:h + 1, 255:256]
        kw = k_v[:, hl].astype(F32) * jnp.exp(total - bc)
        khi, klo = split2(kw)
        vh = v_v[:, hl]
        own = dot(khi, vh, ((0,), (0,))) + dot(klo, vh, ((0,), (0,)))
        st[0, BASE[h]:BASE[h] + HD, :] = own.astype(BF16)
        l1 = total.astype(BF16).astype(F32)
        l2 = (total - l1).astype(BF16).astype(F32)
        for i, term in enumerate((l1, l2, total - l1 - l2)):
            logs = jnp.where(rows16 == 3 * h + i, term, logs)
    st[0, HD:HD + 16, :] = logs.astype(BF16)

    pl.semaphore_wait(barrier, len(others))

    def zcopy(way, h):
        rows = pl.ds(BASE[h], SIZE[h])
        return rcopy(
            st.at[0, rows], st.at[1 + 2 * way, rows], zs.at[way], zr.at[way, h], cdev(1 + 2 * way)
        )

    def zpass(way):
        rows = pl.ds(BASE[way], SIZE[way])
        return rcopy(
            st.at[1 + 2 * way, rows], st.at[2, rows], zs.at[2], zr.at[2, way], cdev(1 + 2 * way)
        )

    wcopy = rcopy(w_hbm, w_all.at[1], wsem.at[0], wsem.at[1], partner)

    zcopy(0, 0).start()
    zcopy(1, 1).start()
    wcopy.start()

    def local_part(h):
        hl = slice(HD * h, HD * h + HD)
        decay = jnp.exp(
            jnp.where(row >= col, bcol[:, h:h + 1] - brow[h:h + 1, :], NEGATIVE)
        )
        scores = dot(q_v[:, hl], k_v[:, hl], ((1,), (1,)))
        weights = (scores * decay).astype(BF16)
        intra_v[h] = dot(weights, v_v[:, hl])

    loads[3].wait()
    local_part(0)
    zcopy(0, 1).start()
    zcopy(1, 0).start()
    local_part(1)
    for i in range(4, 9):
        loads[i].wait()
    pick = (
        lax.broadcasted_iota(jnp.int32, (64, 32), 0) // 2
        == lax.broadcasted_iota(jnp.int32, (64, 32), 1)
    ).astype(F32)
    odd = lax.rem(lax.broadcasted_iota(jnp.int32, (64, 1), 0), 2) == 1
    by_row = ((1,), (1,))
    second = dot(pick, jnp.broadcast_to(prow_v[...], (8, 32)).astype(F32), by_row)[:, 0:1] > 0.5
    dq2 = dqkv_v[0].reshape(64, 256)
    dk2 = dqkv_v[1].astype(F32).reshape(64, 256)
    dv2 = dqkv_v[2].astype(F32).reshape(64, 256)
    cums = []
    for h in range(2):
        hl = slice(HD * h, HD * h + HD)
        rates = dot(pick, dr_v[h], by_row, precision=HIGH)
        step1 = jnp.where(odd, rates[:, 1:2], 0.0)
        cums.append(-rates[:, 0:1] - step1)
        qf, kf, vf = dq2[:, hl].astype(F32), dk2[:, hl], dv2[:, hl]
        same = jnp.sum(qf * kf, axis=-1, keepdims=True)
        before = jnp.sum(qf * pltpu.roll(kf, 1, 0), axis=-1, keepdims=True)
        before = jnp.where(odd, before * jnp.exp(-step1), 0.0)
        dloc_v[h] = same * vf + before * pltpu.roll(vf, 1, 0)

    for way in range(2):
        zcopy(way, way).wait_recv()
        zpass(way).start()
    def state(rel, h):
        s = st[rel, BASE[h]:BASE[h] + HD, :].astype(F32)
        logs = st[rel, HD:HD + 16, :].astype(F32)
        i = 3 * h
        return s, logs[i:i + 1, :] + logs[i + 1:i + 2, :] + logs[i + 2:i + 3, :]

    fcopy = rcopy(fs, fr, fsem.at[0], fsem.at[1], twin)
    hcopy = rcopy(hb.at[1 - c], hb.at[2], hsem.at[0], hsem.at[1], partner)
    dhcopy = rcopy(dhs.at[1 - c], dhr, dhsem.at[0], dhsem.at[1], partner)

    def hidden():
        for way in range(2):
            zcopy(way, 1 - way).wait_recv()
        for way in range(2):
            zpass(way).wait_recv()
        for h in range(2):
            parts = [state(m, h) for m in range(4)]
            total = None
            for m, (s, _) in enumerate(parts):
                cm = lax.rem(ctx - m + 4, 4)
                expo = jnp.zeros((1, HD), F32)
                for n, (_, ln) in enumerate(parts):
                    if n != m:
                        expo = expo + jnp.where(lax.rem(ctx - n + 4, 4) > cm, ln, 0.0)
                term = jnp.exp(expo) * s
                total = term if total is None else total + term
            fs[h] = total.astype(BF16)
        for h in range(2):
            hl = slice(HD * h, HD * h + HD)
            (s1_, l1), (s2_, l2), (s3_, _) = (state(m, h) for m in (1, 2, 3))
            entering = (
                jnp.where(ctx >= 1, 1.0, 0.0) * s1_
                + jnp.where(ctx >= 2, jnp.exp(l1), 0.0) * s2_
                + jnp.where(ctx >= 3, jnp.exp(l1 + l2), 0.0) * s3_
            )
            ehi, elo = split2(entering)
            qh = q_v[:, hl]
            attended = intra_v[h] + jnp.exp(bcol_v[h]) * (dot(qh, ehi) + dot(qh, elo))
            hid = normalize(attended).astype(BF16)
            for s in range(2):
                hb[s, :, hl] = hid[128 * s:128 * s + 128]
            if h == 0:
                fcopy.start()
        hcopy.start()

    def columns(oy, ox):
        jy = lax.rem(y + oy, 4)
        jx = lax.rem(x + ox, 4)
        return pl.ds(pl.multiple_of((jy * 4 + jx) * WIDE, 128), WIDE)

    pl.when(c == 1)(hidden)
    pl.when(c == 0)(hcopy.wait_recv)
    loads[9].wait()
    wcopy.wait_recv()
    first = hb[2 - c]
    for n, (iy, ix) in enumerate(ORDER):
        acc[n] = dot(first, w_all[1 - c, :, columns(OFFS[iy], OFFS[ix])])
    pl.when(c == 0)(hidden)
    pl.when(c == 1)(hcopy.wait_recv)

    def phase1(axis, oi, di):
        if di == 0:
            return rcopy(
                s1.at[axis, oi, 0], rel.at[oi, axis], s1s.at[0], rels.at[oi],
                on_axis(axis, c, 1 if oi % 2 == 0 else 3),
            )
        return rcopy(
            s1.at[axis, oi, di], r1.at[oi, axis, di - 1], s1s.at[0], r1s.at[oi],
            on_axis(axis, c, OFFS[di]),
        )

    later = []

    def flush(new=()):
        for copy in later:
            copy.start()
        later[:] = new

    def project():
        second_h = hb[2 * c]
        held = []
        for n, (iy, ix) in enumerate(ORDER):
            both = acc[n] + dot(second_h, w_all[c, :, columns(OFFS[iy], OFFS[ix])])
            ready = []
            for axis, (oi, di) in enumerate(((iy, ix), (ix, iy))):
                block = both[ROWS * axis:ROWS * axis + ROWS]
                if di == 3:
                    own1[axis, oi] = block
                elif di == 1 + oi % 2:
                    comb[axis, oi] = block
                else:
                    s1[axis, oi, di] = block.astype(BF16)
                    (ready if di == 0 else held).append(phase1(axis, oi, di))
            if n >= len(FIRST):
                ready, held = ready + held, []
            flush(ready)

    def combine(oi):
        di = 1 + oi % 2
        rcopy(s1.at[0, 0:2, 0], rel.at[oi], s1s.at[0], rels.at[oi], partner).wait_recv()
        ready = []
        for axis in range(2):
            both = comb[axis, oi] + rel[oi, axis].astype(F32)
            s1[axis, oi, di] = both.astype(BF16)
            ready.append(phase1(axis, oi, di))
        flush(ready)

    def decode_own(between):
        mine_h = dhs[c]
        for n, (iy, ix) in enumerate(DORDER):
            dacc[n] = dot(mine_h, w_all[0, :, columns(OFFS[iy], OFFS[ix])])
            if n in between:
                between[n]()

    def decode_first(axis, di):
        return rcopy(
            d1s.at[axis, di], d1r.at[axis, di], dsem.at[0], dsem.at[1], on_axis(axis, c, OFFS[di])
        )

    def decode_rest(between):
        part_h = dhr[...]
        left = {(axis, di): 4 for axis in range(2) for di in range(3)}
        for n, (iy, ix) in enumerate(DORDER):
            both = dacc[n] + dot(part_h, w_all[1, :, columns(OFFS[iy], OFFS[ix])])
            ready = []
            for axis, (oi, di) in enumerate(((iy, ix), (ix, iy))):
                block = both[16 * axis:16 * axis + 16]
                if di == 3:
                    down1[axis, oi] = block
                else:
                    d1s[axis, di, oi] = block.astype(BF16)
                    left[axis, di] -= 1
                    if left[axis, di] == 0:
                        ready.append(decode_first(axis, di))
            flush(ready)
            if n in between:
                between[n]()

    def phase2(axis, oi, p):
        return rcopy(
            pk.at[(axis * 3 + oi) * 2 + p], r2.at[(axis * 3 + oi) * 2 + c], psem.at[0], psem.at[1],
            on_axis(1 - axis, p, OFFS[oi]),
        )

    def scatter(oi):
        rcopy(s1.at[:, 0:2, 0], r1.at[oi], s1s.at[0], r1s.at[oi], partner).wait_recv()
        for axis in range(2):
            total = own1[axis, oi] + r1[oi, axis, 0].astype(F32) + r1[oi, axis, 1].astype(F32)
            pa, pb = packed(total)
            if oi < 3:
                slot = (axis * 3 + oi) * 2
                pk[slot] = pa.astype(BF16)
                pk[slot + 1] = pb.astype(BF16)
                flush([phase2(axis, oi, p) for p in range(2)])
            else:
                ownf[axis] = jnp.where(c == 0, pa, pb)
                pk[12 + axis] = jnp.where(c == 0, pb, pa).astype(BF16)
                flush([rcopy(
                    pk.at[12 + axis], r2.at[12 + axis], psem.at[0], psem.at[1], partner
                )])
        flush()

    def decode_scatter():
        all_first = rcopy(d1s, d1r, dsem.at[0], dsem.at[1], partner)
        all_first.wait_recv()
        pad = jnp.zeros((8, HD), F32)
        for oi in range(4):
            for axis in range(2):
                total = down1[axis, oi]
                for di in range(3):
                    total = total + d1r[axis, di, oi].astype(F32)
                pa, pb = (jnp.concatenate([p, pad], axis=0) for p in packed(total))
                if oi < 3:
                    slot = (axis * 3 + oi) * 2
                    dpk[slot] = pa.astype(BF16)
                    dpk[slot + 1] = pb.astype(BF16)
                    flush([
                        rcopy(
                            dpk.at[slot + p], d2r.at[slot + c], dsem.at[2], dsem.at[3],
                            on_axis(1 - axis, p, OFFS[oi]),
                        )
                        for p in range(2)
                    ])
                else:
                    downf[axis] = jnp.where(c == 0, pa, pb)
                    dpk[12 + axis] = jnp.where(c == 0, pb, pa).astype(BF16)
                    flush([rcopy(
                        dpk.at[12 + axis], d2r.at[12 + axis], dsem.at[2], dsem.at[3], partner
                    )])

    project()
    flush()
    fcopy.wait_recv()
    for h in range(2):
        hl = slice(HD * h, HD * h + HD)
        fin = (
            dot(dq2[:, hl], fs[h]),
            dot(dq2[:, hl], fr[h]),
        )
        base = jnp.where(second == (rep == 1), fin[0], fin[1])
        dh = normalize(base * jnp.exp(cums[h]) + dloc_v[h]).astype(BF16)
        for s in range(2):
            dhs[s, :, hl] = dh[32 * s:32 * s + 32]
    flush([dhcopy])
    decode_own({1: flush})
    combine(0)
    flush()
    dhcopy.wait_recv()
    decode_rest({3: lambda: combine(1), 7: lambda: combine(2), 11: lambda: combine(3)})
    for oi in range(3):
        scatter(oi)
    decode_scatter()
    scatter(3)
    flush()
    all_pre = rcopy(pk, r2, psem.at[0], psem.at[1], partner)
    all_pre.wait_recv()
    for axis in range(2):
        for s in range(2):
            total = jnp.where(s == c, ownf[axis], r2[12 + axis].astype(F32))
            for oi in range(3):
                total = total + r2[(axis * 3 + oi) * 2 + s].astype(F32)
            o0, o1 = unpacked(total, c)
            r = ROWS * (2 * s + axis)
            out_ref[r:r + ROWS, 0:128] = o0
            out_ref[r:r + ROWS, 128:192] = o1

    all_dec = rcopy(dpk, d2r, dsem.at[2], dsem.at[3], partner)
    all_dec.wait_recv()
    for axis in range(2):
        for s in range(2):
            total = jnp.where(s == c, downf[axis], d2r[12 + axis].astype(F32))
            for oi in range(3):
                total = total + d2r[(axis * 3 + oi) * 2 + s].astype(F32)
            o0, o1 = unpacked(total[0:24], c)
            r = 16 * (2 * s + axis)
            dec_ref[r:r + 16, 0:128] = o0
            dec_ref[r:r + 16, 128:192] = o1

    wcopy.wait_send()
    for i in range(3):
        rcopy(st.at[0], st.at[2], zs.at[i], zr.at[0, 0], partner).wait_send()
    fcopy.wait_send()
    hcopy.wait_send()
    dhcopy.wait_send()
    rcopy(s1, s1, s1s.at[0], r1s.at[0], partner).wait_send()
    rcopy(d1s, d1r, dsem.at[0], dsem.at[1], partner).wait_send()
    all_dec.wait_send()
    all_pre.wait_send()


def body(pq, pk_, pv, prate, w, dq, dk, dv, drate, prow):
    hbm = pl.BlockSpec(memory_space=pltpu.HBM)
    vmem = pl.BlockSpec(memory_space=pltpu.VMEM)
    dma = pltpu.SemaphoreType.DMA
    out, dec = pl.pallas_call(
        kernel,
        out_shape=(
            pltpu.VMEM((256, 192), BF16),
            pltpu.VMEM((64, 192), BF16),
        ),
        in_specs=[hbm] * 10,
        out_specs=(vmem, vmem),
        scratch_shapes=[
            pltpu.VMEM((256, 256), BF16),
            pltpu.VMEM((256, 256), BF16),
            pltpu.VMEM((256, 256), BF16),
            pltpu.VMEM((2, 256), F32),
            pltpu.VMEM((2, 256, 6144), BF16),
            pltpu.VMEM((3, 32, 2, 256), BF16),
            pltpu.VMEM((2, 2, 32), F32),
            pltpu.VMEM((1, 32), jnp.int32),
            pltpu.VMEM((2, 256, HD), F32),
            pltpu.VMEM((2, 256, HD), F32),
            pltpu.VMEM((2, 64, HD), F32),
            pltpu.VMEM((4, 2 * HD + 16, HD), BF16),
            pltpu.VMEM((2, HD, HD), BF16),
            pltpu.VMEM((2, HD, HD), BF16),
            pltpu.VMEM((3, 2 * ROWS, 256), BF16),
            pltpu.VMEM((16, 2 * ROWS, WIDE), F32),
            pltpu.VMEM((2, 4, 3, ROWS, WIDE), BF16),
            pltpu.VMEM((4, 2, ROWS, WIDE), BF16),
            pltpu.VMEM((4, 2, 2, ROWS, WIDE), BF16),
            pltpu.VMEM((2, 4, ROWS, WIDE), F32),
            pltpu.VMEM((2, 4, ROWS, WIDE), F32),
            pltpu.VMEM((14, PACKED, HD), BF16),
            pltpu.VMEM((2, PACKED, HD), F32),
            pltpu.VMEM((14, PACKED, HD), BF16),
            pltpu.VMEM((2, DROWS, 256), BF16),
            pltpu.VMEM((DROWS, 256), BF16),
            pltpu.VMEM((2, 3, 4, 16, WIDE), BF16),
            pltpu.VMEM((2, 3, 4, 16, WIDE), BF16),
            pltpu.VMEM((16, DROWS, WIDE), F32),
            pltpu.VMEM((2, 4, 16, WIDE), F32),
            pltpu.VMEM((14, 32, HD), BF16),
            pltpu.VMEM((2, 32, HD), F32),
            pltpu.VMEM((14, 32, HD), BF16),
            dma((10,)),
            dma((2,)),
            dma((3,)),
            dma((3, 2)),
            dma((2,)),
            dma((2,)),
            dma((2,)),
            dma((1,)),
            dma((4,)),
            dma((4,)),
            dma((2,)),
            dma((4,)),
        ],
        compiler_params=pltpu.CompilerParams(
            collective_id=0, has_side_effects=True, vmem_limit_bytes=48 << 20
        ),
        name="lightning",
    )(*(pltpu.with_memory_space_constraint(a, pltpu.HBM) for a in (
        pq[0], pk_[0], pv[0], prate[0], w, dq, dk, dv,
        drate.transpose(1, 2, 0), prow.reshape(1, 32),
    )))
    return out[None], dec.reshape(32, 2, 192)


def solution(mesh):
    return jax.shard_map(
        body,
        mesh=mesh,
        in_specs=(
            P("rep", "ctx", "head"),
            P("rep", "ctx", "head"),
            P("rep", "ctx", "head"),
            P("rep", "head", "ctx"),
            P("head", None),
            P(("ctx", "rep"), None, "head"),
            P(("ctx", "rep"), None, "head"),
            P(("ctx", "rep"), None, "head"),
            P(("ctx", "rep"), "head", None),
            P(("ctx", "rep")),
        ),
        out_specs=(P("rep", "ctx", "head"), P(("ctx", "rep"), None, "head")),
        check_vma=False,
    )
```

```python
import jax
import jax.numpy as jnp
from jax import lax
from jax.experimental import pallas as pl
from jax.experimental.pallas import tpu as pltpu
from jax.sharding import PartitionSpec as P

HD = 128
EPSILON = 1e-06
NEGATIVE = -1e30
HIGH = lax.Precision.HIGHEST
MESH = pl.DeviceIdType.MESH
F32 = jnp.float32
BF16 = jnp.bfloat16
OFFS = (2, 1, 3, 0)
FIRST = [(0, 0), (1, 0), (0, 1), (2, 0), (0, 2), (3, 0), (0, 3)]
ORDER = FIRST + [p for p in sorted(
    ((oy, ox) for oy in range(4) for ox in range(4)), key=lambda p: (max(p), p[0] + p[1], p[0])
) if p not in FIRST]
DORDER = FIRST + [(1, 1), (2, 1), (3, 1), (1, 2), (1, 3), (2, 2), (3, 2), (2, 3), (3, 3)]
WIDE = 384
BASE = (0, 144)
SIZE = (144, 128)


def dot(a, b, dims=((1,), (0,)), precision=None):
    return lax.dot_general(
        a, b, (dims, ((), ())), preferred_element_type=F32, precision=precision
    )


def split2(a):
    hi = a.astype(BF16)
    return hi, (a - hi.astype(F32)).astype(BF16)


def normalize(a):
    return a * lax.rsqrt(jnp.mean(a * a, axis=-1, keepdims=True) + EPSILON)


ROWS = 64
DROWS = 32
PACKED = 96


def packed(total):
    half = total.shape[0] // 2
    t0, t1, t2 = (total[:, HD * i:HD * i + HD] for i in range(3))
    top, bottom = t1[0:half], t1[half:]
    lane = lax.broadcasted_iota(jnp.int32, (half, HD), 1)
    ea = jnp.where(lane < 64, top, pltpu.roll(bottom, 64, 1))
    eb = jnp.where(lane < 64, pltpu.roll(top, 64, 1), bottom)
    return jnp.concatenate([t0, ea], axis=0), jnp.concatenate([t2, eb], axis=0)


def unpacked(total, c):
    rows = total.shape[0] * 2 // 3
    main, extra = total[0:rows], total[rows:]
    lane = lax.broadcasted_iota(jnp.int32, (rows, HD), 1)
    ext = jnp.concatenate([extra, pltpu.roll(extra, 64, 1)], axis=0)
    rolled = pltpu.roll(main, 64, 1)
    o0 = jnp.where(c == 0, main, jnp.where(lane < 64, ext, rolled))
    o1 = jnp.where(c == 0, ext, rolled)
    return o0.astype(BF16), o1[:, 0:64].astype(BF16)


def kernel(
    q_hbm, k_hbm, v_hbm, g_hbm, w_hbm, dq_hbm, dk_hbm, dv_hbm, dr_hbm, prow_hbm,
    out_ref, dec_ref,
    q_v, k_v, v_v, g_v, w_all, dqkv_v, dr_v, prow_v,
    intra_v, bcol_v, dloc_v, st, fs, fr,
    hb, acc, s1, rel, r1, comb, own1, pk, ownf, r2, dhs, dhr, d1s, d1r, dacc, down1, dpk, downf, d2r,
    lsem, wsem, zs, zr, fsem, hsem, dhsem, s1s, rels, r1s, psem, dsem,
):
    ctx = lax.axis_index("ctx")
    head = lax.axis_index("head")
    rep = lax.axis_index("rep")
    c = lax.rem(head, 2)
    x = lax.rem(lax.div(head, 2), 4)
    y = lax.div(head, 8)

    def dev(cc, xx, yy):
        return (ctx, (yy * 4 + xx) * 2 + cc, rep)

    def cdev(d):
        return (lax.rem(ctx + d + 4, 4), head, rep)

    partner = dev(1 - c, x, y)
    twin = (ctx, head, 1 - rep)

    def on_axis(axis, cc, d):
        if axis == 0:
            return dev(cc, lax.rem(x + d, 4), y)
        return dev(cc, x, lax.rem(y + d, 4))

    def rcopy(src, dst, ss, rs, device):
        return pltpu.make_async_remote_copy(
            src_ref=src, dst_ref=dst, send_sem=ss, recv_sem=rs,
            device_id=device, device_id_type=MESH,
        )

    loads = [
        pltpu.make_async_copy(a, b, lsem.at[i])
        for i, (a, b) in enumerate(
            ((g_hbm, g_v), (k_hbm, k_v), (v_hbm, v_v), (q_hbm, q_v),
             (dq_hbm, dqkv_v.at[0]), (dk_hbm, dqkv_v.at[1]), (dv_hbm, dqkv_v.at[2]),
             (dr_hbm, dr_v), (prow_hbm, prow_v), (w_hbm, w_all.at[0]))
        )
    ]
    for cp in loads:
        cp.start()

    barrier = pltpu.get_barrier_semaphore()
    others = [partner, twin, cdev(1), cdev(3)]
    others += [on_axis(axis, cc, d) for axis in range(2) for d in (1, 2, 3) for cc in range(2)]
    for device in others:
        pl.semaphore_signal(barrier, inc=1, device_id=device, device_id_type=MESH)

    row = lax.broadcasted_iota(jnp.int32, (256, 256), 0)
    col = lax.broadcasted_iota(jnp.int32, (256, 256), 1)
    lower = (row >= col).astype(F32)
    upper = (row <= col).astype(F32)
    loads[0].wait()
    g = -g_v[...]
    brow = dot(g, upper, precision=HIGH)
    bcol = dot(lower, g, ((1,), (1,)), precision=HIGH)
    loads[1].wait()
    loads[2].wait()
    rows16 = lax.broadcasted_iota(jnp.int32, (16, HD), 0)
    logs = jnp.zeros((16, HD), F32)
    for h in range(2):
        hl = slice(HD * h, HD * h + HD)
        bc = bcol[:, h:h + 1]
        bcol_v[h] = jnp.broadcast_to(bc, (256, HD))
        total = brow[h:h + 1, 255:256]
        kw = k_v[:, hl].astype(F32) * jnp.exp(total - bc)
        khi, klo = split2(kw)
        vh = v_v[:, hl]
        own = dot(khi, vh, ((0,), (0,))) + dot(klo, vh, ((0,), (0,)))
        st[0, BASE[h]:BASE[h] + HD, :] = own.astype(BF16)
        l1 = total.astype(BF16).astype(F32)
        l2 = (total - l1).astype(BF16).astype(F32)
        for i, term in enumerate((l1, l2, total - l1 - l2)):
            logs = jnp.where(rows16 == 3 * h + i, term, logs)
    st[0, HD:HD + 16, :] = logs.astype(BF16)

    pl.semaphore_wait(barrier, len(others))

    def zcopy(way, h):
        rows = pl.ds(BASE[h], SIZE[h])
        return rcopy(
            st.at[0, rows], st.at[1 + 2 * way, rows], zs.at[way], zr.at[way, h], cdev(1 + 2 * way)
        )

    def zpass(way):
        rows = pl.ds(BASE[way], SIZE[way])
        return rcopy(
            st.at[1 + 2 * way, rows], st.at[2, rows], zs.at[2], zr.at[2, way], cdev(1 + 2 * way)
        )

    wcopy = rcopy(w_hbm, w_all.at[1], wsem.at[0], wsem.at[1], partner)

    zcopy(0, 0).start()
    zcopy(1, 1).start()
    wcopy.start()

    def local_part(h):
        hl = slice(HD * h, HD * h + HD)
        decay = jnp.exp(
            jnp.where(row >= col, bcol[:, h:h + 1] - brow[h:h + 1, :], NEGATIVE)
        )
        scores = dot(q_v[:, hl], k_v[:, hl], ((1,), (1,)))
        weights = (scores * decay).astype(BF16)
        intra_v[h] = dot(weights, v_v[:, hl])

    loads[3].wait()
    local_part(0)
    zcopy(0, 1).start()
    zcopy(1, 0).start()
    local_part(1)
    for i in range(4, 9):
        loads[i].wait()
    pick = (
        lax.broadcasted_iota(jnp.int32, (64, 32), 0) // 2
        == lax.broadcasted_iota(jnp.int32, (64, 32), 1)
    ).astype(F32)
    odd = lax.rem(lax.broadcasted_iota(jnp.int32, (64, 1), 0), 2) == 1
    by_row = ((1,), (1,))
    second = dot(pick, jnp.broadcast_to(prow_v[...], (8, 32)).astype(F32), by_row)[:, 0:1] > 0.5
    dq2 = dqkv_v[0].reshape(64, 256)
    dk2 = dqkv_v[1].astype(F32).reshape(64, 256)
    dv2 = dqkv_v[2].astype(F32).reshape(64, 256)
    cums = []
    for h in range(2):
        hl = slice(HD * h, HD * h + HD)
        rates = dot(pick, dr_v[h], by_row, precision=HIGH)
        step1 = jnp.where(odd, rates[:, 1:2], 0.0)
        cums.append(-rates[:, 0:1] - step1)
        qf, kf, vf = dq2[:, hl].astype(F32), dk2[:, hl], dv2[:, hl]
        same = jnp.sum(qf * kf, axis=-1, keepdims=True)
        before = jnp.sum(qf * pltpu.roll(kf, 1, 0), axis=-1, keepdims=True)
        before = jnp.where(odd, before * jnp.exp(-step1), 0.0)
        dloc_v[h] = same * vf + before * pltpu.roll(vf, 1, 0)

    for way in range(2):
        zcopy(way, way).wait_recv()
        zpass(way).start()
    def state(rel, h):
        s = st[rel, BASE[h]:BASE[h] + HD, :].astype(F32)
        logs = st[rel, HD:HD + 16, :].astype(F32)
        i = 3 * h
        return s, logs[i:i + 1, :] + logs[i + 1:i + 2, :] + logs[i + 2:i + 3, :]

    fcopy = rcopy(fs, fr, fsem.at[0], fsem.at[1], twin)
    hcopy = rcopy(hb.at[1 - c], hb.at[2], hsem.at[0], hsem.at[1], partner)
    dhcopy = rcopy(dhs.at[1 - c], dhr, dhsem.at[0], dhsem.at[1], partner)

    def hidden():
        for way in range(2):
            zcopy(way, 1 - way).wait_recv()
        for way in range(2):
            zpass(way).wait_recv()
        for h in range(2):
            parts = [state(m, h) for m in range(4)]
            total = None
            for m, (s, _) in enumerate(parts):
                cm = lax.rem(ctx - m + 4, 4)
                expo = jnp.zeros((1, HD), F32)
                for n, (_, ln) in enumerate(parts):
                    if n != m:
                        expo = expo + jnp.where(lax.rem(ctx - n + 4, 4) > cm, ln, 0.0)
                term = jnp.exp(expo) * s
                total = term if total is None else total + term
            fs[h] = total.astype(BF16)
        for h in range(2):
            hl = slice(HD * h, HD * h + HD)
            (s1_, l1), (s2_, l2), (s3_, _) = (state(m, h) for m in (1, 2, 3))
            entering = (
                jnp.where(ctx >= 1, 1.0, 0.0) * s1_
                + jnp.where(ctx >= 2, jnp.exp(l1), 0.0) * s2_
                + jnp.where(ctx >= 3, jnp.exp(l1 + l2), 0.0) * s3_
            )
            ehi, elo = split2(entering)
            qh = q_v[:, hl]
            attended = intra_v[h] + jnp.exp(bcol_v[h]) * (dot(qh, ehi) + dot(qh, elo))
            hid = normalize(attended).astype(BF16)
            for s in range(2):
                hb[s, :, hl] = hid[128 * s:128 * s + 128]
            if h == 0:
                fcopy.start()
        hcopy.start()

    def columns(oy, ox):
        jy = lax.rem(y + oy, 4)
        jx = lax.rem(x + ox, 4)
        return pl.ds(pl.multiple_of((jy * 4 + jx) * WIDE, 128), WIDE)

    pl.when(c == 1)(hidden)
    pl.when(c == 0)(hcopy.wait_recv)
    loads[9].wait()
    wcopy.wait_recv()
    first = hb[2 - c]
    for n, (iy, ix) in enumerate(ORDER):
        acc[n] = dot(first, w_all[1 - c, :, columns(OFFS[iy], OFFS[ix])])
    pl.when(c == 0)(hidden)
    pl.when(c == 1)(hcopy.wait_recv)

    def phase1(axis, oi, di):
        if di == 0:
            return rcopy(
                s1.at[axis, oi, 0], rel.at[oi, axis], s1s.at[0], rels.at[oi],
                on_axis(axis, c, 1 if oi % 2 == 0 else 3),
            )
        return rcopy(
            s1.at[axis, oi, di], r1.at[oi, axis, di - 1], s1s.at[0], r1s.at[oi],
            on_axis(axis, c, OFFS[di]),
        )

    later = []

    def flush(new=()):
        for copy in later:
            copy.start()
        later[:] = new

    def project():
        second_h = hb[2 * c]
        held = []
        for n, (iy, ix) in enumerate(ORDER):
            both = acc[n] + dot(second_h, w_all[c, :, columns(OFFS[iy], OFFS[ix])])
            ready = []
            for axis, (oi, di) in enumerate(((iy, ix), (ix, iy))):
                block = both[ROWS * axis:ROWS * axis + ROWS]
                if di == 3:
                    own1[axis, oi] = block
                elif di == 1 + oi % 2:
                    comb[axis, oi] = block
                else:
                    s1[axis, oi, di] = block.astype(BF16)
                    (ready if di == 0 else held).append(phase1(axis, oi, di))
            if n >= len(FIRST):
                ready, held = ready + held, []
            flush(ready)

    def combine(oi):
        di = 1 + oi % 2
        rcopy(s1.at[0, 0:2, 0], rel.at[oi], s1s.at[0], rels.at[oi], partner).wait_recv()
        ready = []
        for axis in range(2):
            both = comb[axis, oi] + rel[oi, axis].astype(F32)
            s1[axis, oi, di] = both.astype(BF16)
            ready.append(phase1(axis, oi, di))
        flush(ready)

    def decode_own(between):
        mine_h = dhs[c]
        for n, (iy, ix) in enumerate(DORDER):
            dacc[n] = dot(mine_h, w_all[0, :, columns(OFFS[iy], OFFS[ix])])
            if n in between:
                between[n]()

    def decode_first(axis, di):
        return rcopy(
            d1s.at[axis, di], d1r.at[axis, di], dsem.at[0], dsem.at[1], on_axis(axis, c, OFFS[di])
        )

    def decode_rest(between):
        part_h = dhr[...]
        left = {(axis, di): 4 for axis in range(2) for di in range(3)}
        for n, (iy, ix) in enumerate(DORDER):
            both = dacc[n] + dot(part_h, w_all[1, :, columns(OFFS[iy], OFFS[ix])])
            ready = []
            for axis, (oi, di) in enumerate(((iy, ix), (ix, iy))):
                block = both[16 * axis:16 * axis + 16]
                if di == 3:
                    down1[axis, oi] = block
                else:
                    d1s[axis, di, oi] = block.astype(BF16)
                    left[axis, di] -= 1
                    if left[axis, di] == 0:
                        ready.append(decode_first(axis, di))
            flush(ready)
            if n in between:
                between[n]()

    def phase2(axis, oi, p):
        return rcopy(
            pk.at[(axis * 3 + oi) * 2 + p], r2.at[(axis * 3 + oi) * 2 + c], psem.at[0], psem.at[1],
            on_axis(1 - axis, p, OFFS[oi]),
        )

    def scatter(oi):
        rcopy(s1.at[:, 0:2, 0], r1.at[oi], s1s.at[0], r1s.at[oi], partner).wait_recv()
        for axis in range(2):
            total = own1[axis, oi] + r1[oi, axis, 0].astype(F32) + r1[oi, axis, 1].astype(F32)
            pa, pb = packed(total)
            if oi < 3:
                slot = (axis * 3 + oi) * 2
                pk[slot] = pa.astype(BF16)
                pk[slot + 1] = pb.astype(BF16)
                flush([phase2(axis, oi, p) for p in range(2)])
            else:
                ownf[axis] = jnp.where(c == 0, pa, pb)
                pk[12 + axis] = jnp.where(c == 0, pb, pa).astype(BF16)
                flush([rcopy(
                    pk.at[12 + axis], r2.at[12 + axis], psem.at[0], psem.at[1], partner
                )])
        flush()

    def decode_scatter():
        all_first = rcopy(d1s, d1r, dsem.at[0], dsem.at[1], partner)
        all_first.wait_recv()
        pad = jnp.zeros((8, HD), F32)
        for oi in range(4):
            for axis in range(2):
                total = down1[axis, oi]
                for di in range(3):
                    total = total + d1r[axis, di, oi].astype(F32)
                pa, pb = (jnp.concatenate([p, pad], axis=0) for p in packed(total))
                if oi < 3:
                    slot = (axis * 3 + oi) * 2
                    dpk[slot] = pa.astype(BF16)
                    dpk[slot + 1] = pb.astype(BF16)
                    flush([
                        rcopy(
                            dpk.at[slot + p], d2r.at[slot + c], dsem.at[2], dsem.at[3],
                            on_axis(1 - axis, p, OFFS[oi]),
                        )
                        for p in range(2)
                    ])
                else:
                    downf[axis] = jnp.where(c == 0, pa, pb)
                    dpk[12 + axis] = jnp.where(c == 0, pb, pa).astype(BF16)
                    flush([rcopy(
                        dpk.at[12 + axis], d2r.at[12 + axis], dsem.at[2], dsem.at[3], partner
                    )])

    project()
    flush()
    fcopy.wait_recv()
    for h in range(2):
        hl = slice(HD * h, HD * h + HD)
        fin = (
            dot(dq2[:, hl], fs[h]),
            dot(dq2[:, hl], fr[h]),
        )
        base = jnp.where(second == (rep == 1), fin[0], fin[1])
        dh = normalize(base * jnp.exp(cums[h]) + dloc_v[h]).astype(BF16)
        for s in range(2):
            dhs[s, :, hl] = dh[32 * s:32 * s + 32]
    flush([dhcopy])
    decode_own({1: flush})
    combine(0)
    flush()
    dhcopy.wait_recv()
    decode_rest({3: lambda: combine(1), 7: lambda: combine(2), 11: lambda: combine(3)})
    for oi in range(3):
        scatter(oi)
    scatter(3)
    decode_scatter()
    flush()
    all_pre = rcopy(pk, r2, psem.at[0], psem.at[1], partner)
    all_pre.wait_recv()
    for axis in range(2):
        for s in range(2):
            total = jnp.where(s == c, ownf[axis], r2[12 + axis].astype(F32))
            for oi in range(3):
                total = total + r2[(axis * 3 + oi) * 2 + s].astype(F32)
            o0, o1 = unpacked(total, c)
            r = ROWS * (2 * s + axis)
            out_ref[r:r + ROWS, 0:128] = o0
            out_ref[r:r + ROWS, 128:192] = o1

    all_dec = rcopy(dpk, d2r, dsem.at[2], dsem.at[3], partner)
    all_dec.wait_recv()
    for axis in range(2):
        for s in range(2):
            total = jnp.where(s == c, downf[axis], d2r[12 + axis].astype(F32))
            for oi in range(3):
                total = total + d2r[(axis * 3 + oi) * 2 + s].astype(F32)
            o0, o1 = unpacked(total[0:24], c)
            r = 16 * (2 * s + axis)
            dec_ref[r:r + 16, 0:128] = o0
            dec_ref[r:r + 16, 128:192] = o1

    wcopy.wait_send()
    for i in range(3):
        rcopy(st.at[0], st.at[2], zs.at[i], zr.at[0, 0], partner).wait_send()
    fcopy.wait_send()
    hcopy.wait_send()
    dhcopy.wait_send()
    rcopy(s1, s1, s1s.at[0], r1s.at[0], partner).wait_send()
    rcopy(d1s, d1r, dsem.at[0], dsem.at[1], partner).wait_send()
    all_dec.wait_send()
    all_pre.wait_send()


def body(pq, pk_, pv, prate, w, dq, dk, dv, drate, prow):
    hbm = pl.BlockSpec(memory_space=pltpu.HBM)
    vmem = pl.BlockSpec(memory_space=pltpu.VMEM)
    dma = pltpu.SemaphoreType.DMA
    out, dec = pl.pallas_call(
        kernel,
        out_shape=(
            pltpu.VMEM((256, 192), BF16),
            pltpu.VMEM((64, 192), BF16),
        ),
        in_specs=[hbm] * 10,
        out_specs=(vmem, vmem),
        scratch_shapes=[
            pltpu.VMEM((256, 256), BF16),
            pltpu.VMEM((256, 256), BF16),
            pltpu.VMEM((256, 256), BF16),
            pltpu.VMEM((2, 256), F32),
            pltpu.VMEM((2, 256, 6144), BF16),
            pltpu.VMEM((3, 32, 2, 256), BF16),
            pltpu.VMEM((2, 2, 32), F32),
            pltpu.VMEM((1, 32), jnp.int32),
            pltpu.VMEM((2, 256, HD), F32),
            pltpu.VMEM((2, 256, HD), F32),
            pltpu.VMEM((2, 64, HD), F32),
            pltpu.VMEM((4, 2 * HD + 16, HD), BF16),
            pltpu.VMEM((2, HD, HD), BF16),
            pltpu.VMEM((2, HD, HD), BF16),
            pltpu.VMEM((3, 2 * ROWS, 256), BF16),
            pltpu.VMEM((16, 2 * ROWS, WIDE), F32),
            pltpu.VMEM((2, 4, 3, ROWS, WIDE), BF16),
            pltpu.VMEM((4, 2, ROWS, WIDE), BF16),
            pltpu.VMEM((4, 2, 2, ROWS, WIDE), BF16),
            pltpu.VMEM((2, 4, ROWS, WIDE), F32),
            pltpu.VMEM((2, 4, ROWS, WIDE), F32),
            pltpu.VMEM((14, PACKED, HD), BF16),
            pltpu.VMEM((2, PACKED, HD), F32),
            pltpu.VMEM((14, PACKED, HD), BF16),
            pltpu.VMEM((2, DROWS, 256), BF16),
            pltpu.VMEM((DROWS, 256), BF16),
            pltpu.VMEM((2, 3, 4, 16, WIDE), BF16),
            pltpu.VMEM((2, 3, 4, 16, WIDE), BF16),
            pltpu.VMEM((16, DROWS, WIDE), F32),
            pltpu.VMEM((2, 4, 16, WIDE), F32),
            pltpu.VMEM((14, 32, HD), BF16),
            pltpu.VMEM((2, 32, HD), F32),
            pltpu.VMEM((14, 32, HD), BF16),
            dma((10,)),
            dma((2,)),
            dma((3,)),
            dma((3, 2)),
            dma((2,)),
            dma((2,)),
            dma((2,)),
            dma((1,)),
            dma((4,)),
            dma((4,)),
            dma((2,)),
            dma((4,)),
        ],
        compiler_params=pltpu.CompilerParams(
            collective_id=0, has_side_effects=True, vmem_limit_bytes=48 << 20
        ),
        name="lightning",
    )(*(pltpu.with_memory_space_constraint(a, pltpu.HBM) for a in (
        pq[0], pk_[0], pv[0], prate[0], w, dq, dk, dv,
        drate.transpose(1, 2, 0), prow.reshape(1, 32),
    )))
    return out[None], dec.reshape(32, 2, 192)


def solution(mesh):
    return jax.shard_map(
        body,
        mesh=mesh,
        in_specs=(
            P("rep", "ctx", "head"),
            P("rep", "ctx", "head"),
            P("rep", "ctx", "head"),
            P("rep", "head", "ctx"),
            P("head", None),
            P(("ctx", "rep"), None, "head"),
            P(("ctx", "rep"), None, "head"),
            P(("ctx", "rep"), None, "head"),
            P(("ctx", "rep"), "head", None),
            P(("ctx", "rep")),
        ),
        out_specs=(P("rep", "ctx", "head"), P(("ctx", "rep"), None, "head")),
        check_vma=False,
    )
```
